256 devices in a mesh: grp: 4 (over y), wide: 64 (over z, x, core).
Axes of the slice: x: 4, y: 4, z: 8, core: 2. Of those that a mesh axis runs over, the one named last changes fastest.
Arguments:
- tiles: bfloat16 [12288, 256, 256], P(('grp', 'wide')), may hold values from -0.59765625 to 0.59765625
- contraction: int32 [12288], P(('grp', 'wide')), may hold values from 0 to 15
- row_tile: int32 [12288], P(('grp', 'wide')), may hold values from 0 to 255, as said below
- owner_map: int32 [256], replicated, may hold values from 0 to 255, as said below
- panel: bfloat16 [4096, 768], P('grp'), may hold values from -0.5390625 to 0.5390625
Outputs:
- column_block: float32 [65536, 768], P('wide')
The draws below stay inside these ranges and needn't reach their ends.
Inputs may be any that keep to these rules, and one draw needn't show every extreme that they name: `row_tile`: every row tile's owner is owner_map // 4; among the 48 contributions of one device at most 2 have row tiles of one owner, and on every device some owner gets exactly 2. `owner_map`: A permutation of the row tiles.
All inputs are finite; a program needn't handle non-finite values.
Results may differ from the reference program's by a relative error of at most 0.0003.
Values may be sent and summed in bfloat16 or wider, within the bound.
A program may use at most 192 MiB of HBM per device.

```python
import jax
import jax.numpy as jnp
from jax import lax

TILE = 256
COL_TILES = 3
K_TILES = 16
OUT_DEV = 4
TILE_DEV = 48
MOST = 2
SLOTS = 128
ROW_TILES = 256
CONTRIBS = 12288
N_WIDE = 64


def owner_helper(key):
    base = jax.random.fold_in(key, 5)
    permuted = jax.random.permutation(jax.random.fold_in(base, 1), ROW_TILES).astype(jnp.int32)
    inverse = jnp.zeros((ROW_TILES,), jnp.int32).at[permuted].set(jnp.arange(ROW_TILES, dtype=jnp.int32))
    hotness = jax.random.randint(jax.random.fold_in(base, 2), (N_WIDE,), 0, 4)
    block_count = CONTRIBS // TILE_DEV
    block_keys = jax.random.split(jax.random.fold_in(base, 3), block_count)

    def one_block(block_key):
        first_key, second_key, third_key = jax.random.split(block_key, 3)
        slot_ids = jnp.arange(SLOTS, dtype=jnp.int32)
        owners = slot_ids // MOST
        forced = jax.random.randint(first_key, (), 0, N_WIDE)
        noise = jax.random.randint(second_key, (SLOTS,), 0, 65536)
        scores = noise + hotness[owners] * 16384 + (owners == forced).astype(jnp.int32) * 1048576
        scores = scores * SLOTS + slot_ids
        picked = lax.top_k(scores, TILE_DEV)[1]
        target = picked // MOST
        local_row = jax.random.randint(third_key, (TILE_DEV,), 0, OUT_DEV)
        return inverse[target * OUT_DEV + local_row]
    rows = jax.vmap(one_block)(block_keys).reshape(CONTRIBS).astype(jnp.int32)
    return (permuted, rows)


def draw_row_tile(key, part):
    return owner_helper(key)[1]


def draw_owner_map(key, part):
    return owner_helper(key)[0]


def with_ends(array, stream_key, low, largest):
    longest = array.shape.index(max(array.shape))
    spots = []
    for shift in (0, 1):
        where = [jax.random.randint(jax.random.fold_in(stream_key, axis), (), 0, length) for axis, length in enumerate(array.shape)]
        where[longest] = (where[longest] + shift) % array.shape[longest]
        spots.append(tuple(where))
    return array.at[spots[0]].set(low).at[spots[1]].set(largest)


def block_scale(stream_key, extent, cuts, least, largest):
    level, own = 1.0, jax.random.fold_in(stream_key, 6)
    for dim, blocks in cuts:
        draws = jnp.exp(jax.random.uniform(jax.random.fold_in(own, dim), (blocks,), jnp.float32, least / len(cuts), largest / len(cuts)))
        level = level * jnp.repeat(draws, extent[dim] // blocks).reshape([-1 if axis == dim else 1 for axis in range(len(extent))])
    return level


def centred(rng, shape, spread, reach, cuts=(), kind=jnp.bfloat16):
    result = jax.random.normal(rng, shape, jnp.float32) * spread
    if len(cuts) > 0:
        result = block_scale(rng, shape, cuts, -0.22, 0.18) * result
    return jnp.clip(result, min=-reach, max=reach).astype(kind)


def setup_inputs(seed: int = 0) -> dict:
    splits = jax.random.split(jax.random.key(seed), 6)
    return {
        "tiles": centred(splits[0], (CONTRIBS, TILE, TILE), 0.1, 0.59765625, ((0, 256),)),
        "contraction": with_ends(jax.random.randint(splits[1], (CONTRIBS,), 0, K_TILES), jax.random.fold_in(splits[1], 1), 0, K_TILES - 1).astype(jnp.int32),
        "row_tile": draw_row_tile(jax.random.fold_in(splits[5], 71), 0),
        "owner_map": draw_owner_map(jax.random.fold_in(splits[5], 71), 0),
        "panel": centred(splits[4], (K_TILES * TILE, COL_TILES * TILE), 0.09, 0.5390625, ((0, 4),)),
    }


def reference(tiles, contraction, row_tile, owner_map, panel):
    columns = panel.shape[1]
    panel_tiles = panel.reshape(K_TILES, TILE, columns)
    position = owner_map[row_tile].astype(jnp.int32)
    groups = CONTRIBS // TILE_DEV

    def step(summed, item):
        block_tiles, block_k, block_pos = item
        chosen = panel_tiles[block_k].astype(jnp.float32)
        products = jnp.einsum("sab,sbc->sac", block_tiles.astype(jnp.float32), chosen, precision=lax.Precision.HIGHEST)
        return summed.at[block_pos].add(products), None

    start = jnp.zeros((ROW_TILES, TILE, columns), jnp.float32)
    summed, unused = lax.scan(step, start, (tiles.reshape(groups, TILE_DEV, TILE, TILE), contraction.reshape(groups, TILE_DEV), position.reshape(groups, TILE_DEV)))
    return summed.reshape(ROW_TILES * TILE, columns)
```

```python
import jax
import jax.numpy as jnp
from jax import lax
from jax.experimental import pallas as pl
from jax.experimental.pallas import tpu as pltpu
from jax.sharding import PartitionSpec as P


def place_slots(row_ids, owner_map, out_dev):
    table_ids = jnp.arange(owner_map.shape[0], dtype=jnp.int32)
    position = jnp.sum(jnp.where(row_ids[..., None] == table_ids, owner_map, 0), axis=-1)
    target = position // out_dev
    serial = jnp.arange(row_ids.shape[-1], dtype=jnp.int32)
    earlier = (target[..., :, None] == target[..., None, :]) & (serial[:, None] > serial[None, :])
    ranking = jnp.sum(earlier.astype(jnp.int32), axis=-1)
    return (position % out_dev, target, ranking)


def products_kernel(count_ref, order_ref, rows_ref, ks_ref, arrived_hbm, panel_ref, out_ref, buf, sem):
    out_ref[...] = jnp.zeros_like(out_ref)
    count = count_ref[0]
    columns = panel_ref.shape[2]
    side = buf.shape[2]

    def fetch(i, slot):
        return pltpu.make_async_copy(arrived_hbm.at[order_ref[i]], buf.at[slot], sem.at[slot])

    @pl.when(count > 0)
    def _():
        fetch(0, 0).start()

    def body(i, carry):
        slot = i % 2

        @pl.when(i + 1 < count)
        def _():
            fetch(i + 1, 1 - slot).start()

        fetch(i, slot).wait()
        source = order_ref[i]
        row = rows_ref[source]
        k = ks_ref[source]
        tile = buf[slot]
        for c in range(columns // side):
            cols = pl.ds(c * side, side)
            out_ref[row, :, cols] += jnp.dot(
                tile, panel_ref[k, :, cols], preferred_element_type=jnp.float32
            )
        return carry

    lax.fori_loop(0, count, body, 0)


def add_products(arrived, arrived_labels, panel_tiles, out_dev):
    slot_count, side = arrived.shape[0], arrived.shape[1]
    rows = arrived_labels[:, 0]
    ks = arrived_labels[:, 1]
    vacant = (rows >= out_dev).astype(jnp.int32)
    order = jnp.argsort(vacant, stable=True).astype(jnp.int32)
    count = jnp.reshape(slot_count - jnp.sum(vacant), (1,)).astype(jnp.int32)
    smem = pl.BlockSpec(memory_space=pltpu.SMEM)
    return pl.pallas_call(
        products_kernel,
        out_shape=jax.ShapeDtypeStruct((out_dev, side, panel_tiles.shape[2]), jnp.float32),
        in_specs=[smem, smem, smem, smem,
                  pl.BlockSpec(memory_space=pl.ANY),
                  pl.BlockSpec(memory_space=pltpu.VMEM)],
        out_specs=pl.BlockSpec(memory_space=pltpu.VMEM),
        scratch_shapes=[
            pltpu.VMEM((2, side, side), arrived.dtype),
            pltpu.SemaphoreType.DMA((2,)),
        ],
        compiler_params=pltpu.CompilerParams(vmem_limit_bytes=48 * 1024 * 1024),
    )(count, order, rows, ks, arrived, panel_tiles)


def per_device(tiles, contraction, row_tile, owner_map, panel):
    wide_count = lax.axis_size("wide")
    tile_dev = tiles.shape[0]
    tile_side = tiles.shape[1]
    out_dev = owner_map.shape[0] // wide_count
    most_slots = tile_dev * 8 // (3 * wide_count)
    slot_total = wide_count * most_slots
    local_row, target, ranking = place_slots(row_tile, owner_map, out_dev)
    slot_index = target * most_slots + ranking
    outgoing = jnp.zeros((slot_total, tile_side, tile_side), tiles.dtype).at[slot_index].set(tiles)
    vacant_label = jnp.stack(
        [jnp.full((slot_total,), out_dev, jnp.int32), jnp.zeros((slot_total,), jnp.int32)], axis=1
    )
    label_out = vacant_label.at[slot_index].set(jnp.stack([local_row, contraction], axis=1))
    arrived_labels = lax.all_to_all(label_out, "wide", split_axis=0, concat_axis=0, tiled=True)
    gathered = lax.all_gather(panel, "grp", axis=0, tiled=True)
    panel_tiles = gathered.reshape(gathered.shape[0] // tile_side, tile_side, gathered.shape[1])
    arrived = lax.all_to_all(outgoing, "wide", split_axis=0, concat_axis=0, tiled=True)
    summed = add_products(arrived, arrived_labels, panel_tiles, out_dev)
    summed = lax.psum(summed, "grp")
    return summed.reshape(out_dev * tile_side, gathered.shape[1])


def solution(mesh):
    return jax.shard_map(
        per_device,
        mesh=mesh,
        in_specs=(
            P(("grp", "wide"), None, None),
            P(("grp", "wide")),
            P(("grp", "wide")),
            P(),
            P("grp", None),
        ),
        out_specs=P("wide", None),
        check_vma=False,
    )
```

```python
import jax
import jax.numpy as jnp
from jax import lax
from jax.experimental import pallas as pl
from jax.experimental.pallas import tpu as pltpu
from jax.sharding import PartitionSpec as P


def place_slots(row_ids, owner_map, out_dev):
    table_ids = jnp.arange(owner_map.shape[0], dtype=jnp.int32)
    position = jnp.sum(jnp.where(row_ids[..., None] == table_ids, owner_map, 0), axis=-1)
    target = position // out_dev
    serial = jnp.arange(row_ids.shape[-1], dtype=jnp.int32)
    earlier = (target[..., :, None] == target[..., None, :]) & (serial[:, None] > serial[None, :])
    ranking = jnp.sum(earlier.astype(jnp.int32), axis=-1)
    return (position % out_dev, target, ranking)


def products_kernel(count_ref, order_ref, rows_ref, ks_ref, arrived_hbm, panel_ref, init_ref, out_ref, buf, sem):
    out_ref[...] = init_ref[...]
    count = count_ref[0]
    columns = panel_ref.shape[2]
    side = buf.shape[2]

    def fetch(i, slot):
        return pltpu.make_async_copy(arrived_hbm.at[order_ref[i]], buf.at[slot], sem.at[slot])

    @pl.when(count > 0)
    def _():
        fetch(0, 0).start()

    def body(i, carry):
        slot = i % 2

        @pl.when(i + 1 < count)
        def _():
            fetch(i + 1, 1 - slot).start()

        fetch(i, slot).wait()
        source = order_ref[i]
        row = rows_ref[source]
        k = ks_ref[source]
        tile = buf[slot]
        for c in range(columns // side):
            cols = pl.ds(c * side, side)
            out_ref[row, :, cols] += jnp.dot(
                tile, panel_ref[k, :, cols], preferred_element_type=jnp.float32
            )
        return carry

    lax.fori_loop(0, count, body, 0)


def add_products(arrived, arrived_labels, panel_tiles, running):
    slot_count, side = arrived.shape[0], arrived.shape[1]
    out_dev = running.shape[0]
    rows = arrived_labels[:, 0]
    ks = arrived_labels[:, 1]
    vacant = (rows >= out_dev).astype(jnp.int32)
    order = jnp.argsort(vacant, stable=True).astype(jnp.int32)
    count = jnp.reshape(slot_count - jnp.sum(vacant), (1,)).astype(jnp.int32)
    smem = pl.BlockSpec(memory_space=pltpu.SMEM)
    return pl.pallas_call(
        products_kernel,
        out_shape=jax.ShapeDtypeStruct((out_dev, side, panel_tiles.shape[2]), jnp.float32),
        in_specs=[smem, smem, smem, smem,
                  pl.BlockSpec(memory_space=pl.ANY),
                  pl.BlockSpec(memory_space=pltpu.VMEM),
                  pl.BlockSpec(memory_space=pltpu.VMEM)],
        out_specs=pl.BlockSpec(memory_space=pltpu.VMEM),
        scratch_shapes=[
            pltpu.VMEM((2, side, side), arrived.dtype),
            pltpu.SemaphoreType.DMA((2,)),
        ],
        compiler_params=pltpu.CompilerParams(vmem_limit_bytes=48 * 1024 * 1024),
    )(count, order, rows, ks, arrived, panel_tiles, running)


def per_device(tiles, contraction, row_tile, owner_map, panel):
    wide_count = lax.axis_size("wide")
    tile_dev = tiles.shape[0]
    tile_side = tiles.shape[1]
    out_dev = owner_map.shape[0] // wide_count
    most_slots = tile_dev * 8 // (3 * wide_count)
    slot_total = wide_count * most_slots
    local_row, target, ranking = place_slots(row_tile, owner_map, out_dev)
    slot_index = target * most_slots + ranking
    vacant_label = jnp.stack(
        [jnp.full((slot_total,), out_dev, jnp.int32), jnp.zeros((slot_total,), jnp.int32)], axis=1
    )
    label_out = vacant_label.at[slot_index].set(jnp.stack([local_row, contraction], axis=1))
    arrived_labels = lax.all_to_all(label_out, "wide", split_axis=0, concat_axis=0, tiled=True)
    arrived_labels = arrived_labels.reshape(wide_count, most_slots, 2)
    gathered = lax.all_gather(panel, "grp", axis=0, tiled=True)
    panel_tiles = gathered.reshape(gathered.shape[0] // tile_side, tile_side, gathered.shape[1])
    summed = jnp.zeros((out_dev, tile_side, gathered.shape[1]), jnp.float32)
    for rank in range(most_slots):
        chunk_index = jnp.where(ranking == rank, target, wide_count)
        outgoing = jnp.zeros((wide_count, tile_side, tile_side), tiles.dtype).at[chunk_index].set(
            tiles, mode="drop"
        )
        arrived = lax.all_to_all(outgoing, "wide", split_axis=0, concat_axis=0, tiled=True)
        summed = add_products(arrived, arrived_labels[:, rank, :], panel_tiles, summed)
    summed = lax.psum(summed, "grp")
    return summed.reshape(out_dev * tile_side, gathered.shape[1])


def solution(mesh):
    return jax.shard_map(
        per_device,
        mesh=mesh,
        in_specs=(
            P(("grp", "wide"), None, None),
            P(("grp", "wide")),
            P(("grp", "wide")),
            P(),
            P("grp", None),
        ),
        out_specs=P("wide", None),
        check_vma=False,
    )
```

```python
import jax
import jax.numpy as jnp
from jax import lax
from jax.experimental import pallas as pl
from jax.experimental.pallas import tpu as pltpu
from jax.sharding import PartitionSpec as P

ROW_BANDS = 4


def place_slots(row_ids, owner_map, out_dev):
    table_ids = jnp.arange(owner_map.shape[0], dtype=jnp.int32)
    position = jnp.sum(jnp.where(row_ids[..., None] == table_ids, owner_map, 0), axis=-1)
    target = position // out_dev
    serial = jnp.arange(row_ids.shape[-1], dtype=jnp.int32)
    earlier = (target[..., :, None] == target[..., None, :]) & (serial[:, None] > serial[None, :])
    ranking = jnp.sum(earlier.astype(jnp.int32), axis=-1)
    return (position % out_dev, target, ranking)


def products_kernel(count_ref, order_ref, rows_ref, ks_ref, arrived_hbm, panel_ref, out_ref, buf, sem):
    out_ref[...] = jnp.zeros_like(out_ref)
    count = count_ref[0]
    columns = panel_ref.shape[2]
    side = buf.shape[2]

    def fetch(i, slot):
        return pltpu.make_async_copy(arrived_hbm.at[order_ref[i]], buf.at[slot], sem.at[slot])

    @pl.when(count > 0)
    def _():
        fetch(0, 0).start()

    def body(i, carry):
        slot = i % 2

        @pl.when(i + 1 < count)
        def _():
            fetch(i + 1, 1 - slot).start()

        fetch(i, slot).wait()
        source = order_ref[i]
        row = rows_ref[source]
        k = ks_ref[source]
        tile = buf[slot]
        for c in range(columns // side):
            cols = pl.ds(c * side, side)
            out_ref[row, :, cols] += jnp.dot(
                tile, panel_ref[k, :, cols], preferred_element_type=jnp.float32
            )
        return carry

    lax.fori_loop(0, count, body, 0)


def add_products(arrived, count, order, rows, ks, panel_tiles, out_dev):
    side = arrived.shape[2]
    smem = pl.BlockSpec(memory_space=pltpu.SMEM)
    return pl.pallas_call(
        products_kernel,
        out_shape=jax.ShapeDtypeStruct((out_dev, arrived.shape[1], panel_tiles.shape[2]), jnp.float32),
        in_specs=[smem, smem, smem, smem,
                  pl.BlockSpec(memory_space=pl.ANY),
                  pl.BlockSpec(memory_space=pltpu.VMEM)],
        out_specs=pl.BlockSpec(memory_space=pltpu.VMEM),
        scratch_shapes=[
            pltpu.VMEM((2, arrived.shape[1], side), arrived.dtype),
            pltpu.SemaphoreType.DMA((2,)),
        ],
        compiler_params=pltpu.CompilerParams(vmem_limit_bytes=48 * 1024 * 1024),
    )(count, order, rows, ks, arrived, panel_tiles)


def per_device(tiles, contraction, row_tile, owner_map, panel):
    wide_count = lax.axis_size("wide")
    tile_dev = tiles.shape[0]
    tile_side = tiles.shape[1]
    out_dev = owner_map.shape[0] // wide_count
    most_slots = tile_dev * 8 // (3 * wide_count)
    slot_total = wide_count * most_slots
    local_row, target, ranking = place_slots(row_tile, owner_map, out_dev)
    slot_index = target * most_slots + ranking
    vacant_label = jnp.stack(
        [jnp.full((slot_total,), out_dev, jnp.int32), jnp.zeros((slot_total,), jnp.int32)], axis=1
    )
    label_out = vacant_label.at[slot_index].set(jnp.stack([local_row, contraction], axis=1))
    arrived_labels = lax.all_to_all(label_out, "wide", split_axis=0, concat_axis=0, tiled=True)
    rows = arrived_labels[:, 0]
    ks = arrived_labels[:, 1]
    vacant = (rows >= out_dev).astype(jnp.int32)
    order = jnp.argsort(vacant, stable=True).astype(jnp.int32)
    count = jnp.reshape(slot_total - jnp.sum(vacant), (1,)).astype(jnp.int32)
    gathered = lax.all_gather(panel, "grp", axis=0, tiled=True)
    panel_tiles = gathered.reshape(gathered.shape[0] // tile_side, tile_side, gathered.shape[1])
    band = tile_side // ROW_BANDS
    pieces = []
    raw = []
    for which in range(ROW_BANDS):
        outgoing = jnp.zeros((slot_total, band, tile_side), tiles.dtype).at[slot_index].set(
            tiles[:, which * band:(which + 1) * band, :]
        )
        if which >= 2:
            outgoing, raw[which - 2] = lax.optimization_barrier((outgoing, raw[which - 2]))
        arrived = lax.all_to_all(outgoing, "wide", split_axis=0, concat_axis=0, tiled=True)
        raw.append(add_products(arrived, count, order, rows, ks, panel_tiles, out_dev))
    for which in range(ROW_BANDS):
        piece = raw[which]
        if pieces:
            piece, pieces[-1] = lax.optimization_barrier((piece, pieces[-1]))
        pieces.append(lax.psum(piece, "grp"))
    summed = jnp.concatenate(pieces, axis=1)
    return summed.reshape(out_dev * tile_side, gathered.shape[1])


def solution(mesh):
    return jax.shard_map(
        per_device,
        mesh=mesh,
        in_specs=(
            P(("grp", "wide"), None, None),
            P(("grp", "wide")),
            P(("grp", "wide")),
            P(),
            P("grp", None),
        ),
        out_specs=P("wide", None),
        check_vma=False,
    )
```

```python
import jax
import jax.numpy as jnp
from jax import lax
from jax.experimental import pallas as pl
from jax.experimental.pallas import tpu as pltpu
from jax.sharding import PartitionSpec as P


def place_slots(row_ids, owner_map, out_dev):
    table_ids = jnp.arange(owner_map.shape[0], dtype=jnp.int32)
    position = jnp.sum(jnp.where(row_ids[..., None] == table_ids, owner_map, 0), axis=-1)
    target = position // out_dev
    serial = jnp.arange(row_ids.shape[-1], dtype=jnp.int32)
    earlier = (target[..., :, None] == target[..., None, :]) & (serial[:, None] > serial[None, :])
    ranking = jnp.sum(earlier.astype(jnp.int32), axis=-1)
    return (position % out_dev, target, ranking)


def products_kernel(count_ref, order_ref, rows_ref, ks_ref, arrived_ref, panel_ref, init_ref, out_ref):
    out_ref[...] = init_ref[...]
    columns = panel_ref.shape[2]
    side = arrived_ref.shape[2]

    def body(i, carry):
        source = order_ref[i]
        row = rows_ref[source]
        k = ks_ref[source]
        tile = arrived_ref[source]
        for c in range(columns // side):
            cols = pl.ds(c * side, side)
            out_ref[row, :, cols] += jnp.dot(
                tile, panel_ref[k, :, cols], preferred_element_type=jnp.float32
            )
        return carry

    lax.fori_loop(0, count_ref[0], body, 0)


def add_products(arrived, arrived_labels, panel_tiles, running):
    slot_count, side = arrived.shape[0], arrived.shape[1]
    out_dev = running.shape[0]
    rows = arrived_labels[:, 0]
    ks = arrived_labels[:, 1]
    vacant = (rows >= out_dev).astype(jnp.int32)
    order = jnp.argsort(vacant, stable=True).astype(jnp.int32)
    count = jnp.reshape(slot_count - jnp.sum(vacant), (1,)).astype(jnp.int32)
    smem = pl.BlockSpec(memory_space=pltpu.SMEM)
    return pl.pallas_call(
        products_kernel,
        out_shape=jax.ShapeDtypeStruct((out_dev, side, panel_tiles.shape[2]), jnp.float32),
        in_specs=[smem, smem, smem, smem,
                  pl.BlockSpec(memory_space=pltpu.VMEM),
                  pl.BlockSpec(memory_space=pltpu.VMEM),
                  pl.BlockSpec(memory_space=pltpu.VMEM)],
        out_specs=pl.BlockSpec(memory_space=pltpu.VMEM),
        compiler_params=pltpu.CompilerParams(vmem_limit_bytes=48 * 1024 * 1024),
    )(count, order, rows, ks, arrived, panel_tiles, running)


def per_device(tiles, contraction, row_tile, owner_map, panel):
    wide_count = lax.axis_size("wide")
    tile_dev = tiles.shape[0]
    tile_side = tiles.shape[1]
    out_dev = owner_map.shape[0] // wide_count
    most_slots = tile_dev * 8 // (3 * wide_count)
    slot_total = wide_count * most_slots
    local_row, target, ranking = place_slots(row_tile, owner_map, out_dev)
    slot_index = target * most_slots + ranking
    vacant_label = jnp.stack(
        [jnp.full((slot_total,), out_dev, jnp.int32), jnp.zeros((slot_total,), jnp.int32)], axis=1
    )
    label_out = vacant_label.at[slot_index].set(jnp.stack([local_row, contraction], axis=1))
    arrived_labels = lax.all_to_all(label_out, "wide", split_axis=0, concat_axis=0, tiled=True)
    arrived_labels = arrived_labels.reshape(wide_count, most_slots, 2)
    gathered = lax.all_gather(panel, "grp", axis=0, tiled=True)
    panel_tiles = gathered.reshape(gathered.shape[0] // tile_side, tile_side, gathered.shape[1])
    summed = jnp.zeros((out_dev, tile_side, gathered.shape[1]), jnp.float32)
    for rank in range(most_slots):
        chunk_index = jnp.where(ranking == rank, target, wide_count)
        picks = jnp.full((wide_count,), tile_dev, jnp.int32).at[chunk_index].set(
            jnp.arange(tile_dev, dtype=jnp.int32), mode="drop"
        )
        outgoing = jnp.take(tiles, picks, axis=0, mode="fill", fill_value=0)
        arrived = lax.all_to_all(outgoing, "wide", split_axis=0, concat_axis=0, tiled=True)
        summed = add_products(arrived, arrived_labels[:, rank, :], panel_tiles, summed)
    summed = lax.psum(summed, "grp")
    return summed.reshape(out_dev * tile_side, gathered.shape[1])


def solution(mesh):
    return jax.shard_map(
        per_device,
        mesh=mesh,
        in_specs=(
            P(("grp", "wide"), None, None),
            P(("grp", "wide")),
            P(("grp", "wide")),
            P(),
            P("grp", None),
        ),
        out_specs=P("wide", None),
        check_vma=False,
    )
```

```python
import jax
import jax.numpy as jnp
from jax import lax
from jax.experimental import pallas as pl
from jax.experimental.pallas import tpu as pltpu
from jax.sharding import PartitionSpec as P


def place_slots(row_ids, owner_map, out_dev):
    table_ids = jnp.arange(owner_map.shape[0], dtype=jnp.int32)
    position = jnp.sum(jnp.where(row_ids[..., None] == table_ids, owner_map, 0), axis=-1)
    target = position // out_dev
    serial = jnp.arange(row_ids.shape[-1], dtype=jnp.int32)
    earlier = (target[..., :, None] == target[..., None, :]) & (serial[:, None] > serial[None, :])
    ranking = jnp.sum(earlier.astype(jnp.int32), axis=-1)
    return (position % out_dev, target, ranking)


def products_kernel(count_ref, order_ref, rows_ref, ks_ref, arrived_ref, panel_ref, init_ref, out_ref):
    out_ref[...] = init_ref[...]
    columns = panel_ref.shape[2]
    side = arrived_ref.shape[2]

    def body(i, carry):
        source = order_ref[i]
        row = rows_ref[source]
        k = ks_ref[source]
        tile = arrived_ref[source]
        for c in range(columns // side):
            cols = pl.ds(c * side, side)
            out_ref[row, :, cols] += jnp.dot(
                tile, panel_ref[k, :, cols], preferred_element_type=jnp.float32
            )
        return carry

    lax.fori_loop(0, count_ref[0], body, 0)


def add_products(arrived, arrived_labels, panel_tiles, running):
    slot_count, side = arrived.shape[0], arrived.shape[1]
    out_dev = running.shape[0]
    rows = arrived_labels[:, 0]
    ks = arrived_labels[:, 1]
    vacant = (rows >= out_dev).astype(jnp.int32)
    order = jnp.argsort(vacant, stable=True).astype(jnp.int32)
    count = jnp.reshape(slot_count - jnp.sum(vacant), (1,)).astype(jnp.int32)
    smem = pl.BlockSpec(memory_space=pltpu.SMEM)
    return pl.pallas_call(
        products_kernel,
        out_shape=jax.ShapeDtypeStruct((out_dev, side, panel_tiles.shape[2]), jnp.float32),
        in_specs=[smem, smem, smem, smem,
                  pl.BlockSpec(memory_space=pltpu.VMEM),
                  pl.BlockSpec(memory_space=pltpu.VMEM),
                  pl.BlockSpec(memory_space=pltpu.VMEM)],
        out_specs=pl.BlockSpec(memory_space=pltpu.VMEM),
        compiler_params=pltpu.CompilerParams(vmem_limit_bytes=48 * 1024 * 1024),
    )(count, order, rows, ks, arrived, panel_tiles, running)


def per_device(tiles, contraction, row_tile, owner_map, panel):
    wide_count = lax.axis_size("wide")
    tile_dev = tiles.shape[0]
    tile_side = tiles.shape[1]
    out_dev = owner_map.shape[0] // wide_count
    most_slots = tile_dev * 8 // (3 * wide_count)
    slot_total = wide_count * most_slots
    local_row, target, ranking = place_slots(row_tile, owner_map, out_dev)
    slot_index = target * most_slots + ranking
    vacant_label = jnp.stack(
        [jnp.full((slot_total,), out_dev, jnp.int32), jnp.zeros((slot_total,), jnp.int32)], axis=1
    )
    label_out = vacant_label.at[slot_index].set(jnp.stack([local_row, contraction], axis=1))
    arrived_labels = lax.all_to_all(label_out, "wide", split_axis=0, concat_axis=0, tiled=True)
    arrived_labels = arrived_labels.reshape(wide_count, most_slots, 2)
    gathered = lax.all_gather(panel, "grp", axis=0, tiled=True)
    panel_tiles = gathered.reshape(gathered.shape[0] // tile_side, tile_side, gathered.shape[1])
    summed = jnp.zeros((out_dev, tile_side, gathered.shape[1]), jnp.float32)
    for rank in range(most_slots):
        chunk_index = jnp.where(ranking == rank, target, wide_count)
        picks = jnp.full((wide_count,), tile_dev, jnp.int32).at[chunk_index].set(
            jnp.arange(tile_dev, dtype=jnp.int32), mode="drop"
        )
        outgoing = jnp.take(tiles, picks, axis=0, mode="clip")
        arrived = lax.all_to_all(outgoing, "wide", split_axis=0, concat_axis=0, tiled=True)
        summed = add_products(arrived, arrived_labels[:, rank, :], panel_tiles, summed)
    summed = lax.psum(summed, "grp")
    return summed.reshape(out_dev * tile_side, gathered.shape[1])


def solution(mesh):
    return jax.shard_map(
        per_device,
        mesh=mesh,
        in_specs=(
            P(("grp", "wide"), None, None),
            P(("grp", "wide")),
            P(("grp", "wide")),
            P(),
            P("grp", None),
        ),
        out_specs=P("wide", None),
        check_vma=False,
    )
```

```python
import functools

import jax
import jax.numpy as jnp
from jax import lax
from jax.experimental import pallas as pl
from jax.experimental.pallas import tpu as pltpu
from jax.sharding import PartitionSpec as P


MESH = pl.DeviceIdType.MESH


def ring_sum_kernel(n, x_ref, out_ref, sbuf, rbuf, send_sem, recv_sem):
    me = lax.axis_index("grp")
    column = lax.axis_index("wide")
    right = lax.rem(me + 1, n)
    left = lax.rem(me + n - 1, n)
    half = x_ref.shape[1] // 2
    neighbours = (right, left)

    barrier = pltpu.get_barrier_semaphore()
    for neighbour in (left, right):
        pl.semaphore_signal(barrier, inc=1, device_id=(neighbour, column), device_id_type=MESH)
    pl.semaphore_wait(barrier, 2)

    def send(way, step, src, dst):
        copy = pltpu.make_async_remote_copy(
            src_ref=src,
            dst_ref=dst,
            send_sem=send_sem.at[way, step],
            recv_sem=recv_sem.at[way, step],
            device_id=(neighbours[way], column),
            device_id_type=MESH,
        )
        copy.start()
        return copy

    for step in range(n - 1):
        copies = []
        for way in range(2):
            sign = 1 - 2 * way
            rows = pl.ds(way * half, half)
            chunk = lax.rem(me - sign * (step + 1) + 2 * n, n)
            if step == 0:
                src = x_ref.at[chunk, rows]
            else:
                sbuf[way, step] = rbuf[way, step - 1] + x_ref[chunk, rows]
                src = sbuf.at[way, step]
            copies.append(send(way, step, src, rbuf.at[way, step]))
        for copy in copies:
            copy.wait()

    for way in range(2):
        rows = pl.ds(way * half, half)
        out_ref[me, rows] = rbuf[way, n - 2] + x_ref[me, rows]

    for step in range(n - 1):
        copies = []
        for way in range(2):
            sign = 1 - 2 * way
            rows = pl.ds(way * half, half)
            chunk = lax.rem(me - sign * step + 2 * n, n)
            copies.append(send(way, n - 1 + step, out_ref.at[chunk, rows], out_ref.at[chunk, rows]))
        for copy in copies:
            copy.wait()


def ring_sum(x, n):
    half = x.shape[1] // 2
    return pl.pallas_call(
        functools.partial(ring_sum_kernel, n),
        out_shape=jax.ShapeDtypeStruct(x.shape, x.dtype),
        in_specs=[pl.BlockSpec(memory_space=pltpu.VMEM)],
        out_specs=pl.BlockSpec(memory_space=pltpu.VMEM),
        scratch_shapes=[
            pltpu.VMEM((2, n - 1, half, x.shape[2]), x.dtype),
            pltpu.VMEM((2, n - 1, half, x.shape[2]), x.dtype),
            pltpu.SemaphoreType.DMA((2, 2 * (n - 1))),
            pltpu.SemaphoreType.DMA((2, 2 * (n - 1))),
        ],
        compiler_params=pltpu.CompilerParams(
            collective_id=0, has_side_effects=True, vmem_limit_bytes=48 * 1024 * 1024
        ),
    )(x)


def place_slots(row_ids, owner_map, out_dev):
    table_ids = jnp.arange(owner_map.shape[0], dtype=jnp.int32)
    position = jnp.sum(jnp.where(row_ids[..., None] == table_ids, owner_map, 0), axis=-1)
    target = position // out_dev
    serial = jnp.arange(row_ids.shape[-1], dtype=jnp.int32)
    earlier = (target[..., :, None] == target[..., None, :]) & (serial[:, None] > serial[None, :])
    ranking = jnp.sum(earlier.astype(jnp.int32), axis=-1)
    return (position % out_dev, target, ranking)


def products_kernel(count_ref, order_ref, rows_ref, ks_ref, arrived_ref, panel_ref, init_ref, out_ref):
    out_ref[...] = init_ref[...]
    columns = panel_ref.shape[2]
    side = arrived_ref.shape[2]

    def body(i, carry):
        source = order_ref[i]
        row = rows_ref[source]
        k = ks_ref[source]
        tile = arrived_ref[source]
        for c in range(columns // side):
            cols = pl.ds(c * side, side)
            out_ref[row, :, cols] += jnp.dot(
                tile, panel_ref[k, :, cols], preferred_element_type=jnp.float32
            )
        return carry

    lax.fori_loop(0, count_ref[0], body, 0)


def add_products(arrived, arrived_labels, panel_tiles, running):
    slot_count, side = arrived.shape[0], arrived.shape[1]
    out_dev = running.shape[0]
    rows = arrived_labels[:, 0]
    ks = arrived_labels[:, 1]
    vacant = (rows >= out_dev).astype(jnp.int32)
    order = jnp.argsort(vacant, stable=True).astype(jnp.int32)
    count = jnp.reshape(slot_count - jnp.sum(vacant), (1,)).astype(jnp.int32)
    smem = pl.BlockSpec(memory_space=pltpu.SMEM)
    return pl.pallas_call(
        products_kernel,
        out_shape=jax.ShapeDtypeStruct((out_dev, side, panel_tiles.shape[2]), jnp.float32),
        in_specs=[smem, smem, smem, smem,
                  pl.BlockSpec(memory_space=pltpu.VMEM),
                  pl.BlockSpec(memory_space=pltpu.VMEM),
                  pl.BlockSpec(memory_space=pltpu.VMEM)],
        out_specs=pl.BlockSpec(memory_space=pltpu.VMEM),
        compiler_params=pltpu.CompilerParams(vmem_limit_bytes=48 * 1024 * 1024),
    )(count, order, rows, ks, arrived, panel_tiles, running)


def per_device(tiles, contraction, row_tile, owner_map, panel):
    wide_count = lax.axis_size("wide")
    tile_dev = tiles.shape[0]
    tile_side = tiles.shape[1]
    out_dev = owner_map.shape[0] // wide_count
    most_slots = tile_dev * 8 // (3 * wide_count)
    slot_total = wide_count * most_slots
    local_row, target, ranking = place_slots(row_tile, owner_map, out_dev)
    slot_index = target * most_slots + ranking
    vacant_label = jnp.stack(
        [jnp.full((slot_total,), out_dev, jnp.int32), jnp.zeros((slot_total,), jnp.int32)], axis=1
    )
    label_out = vacant_label.at[slot_index].set(jnp.stack([local_row, contraction], axis=1))
    arrived_labels = lax.all_to_all(label_out, "wide", split_axis=0, concat_axis=0, tiled=True)
    arrived_labels = arrived_labels.reshape(wide_count, most_slots, 2)
    gathered = lax.all_gather(panel, "grp", axis=0, tiled=True)
    panel_tiles = gathered.reshape(gathered.shape[0] // tile_side, tile_side, gathered.shape[1])
    summed = jnp.zeros((out_dev, tile_side, gathered.shape[1]), jnp.float32)
    for rank in range(most_slots):
        chunk_index = jnp.where(ranking == rank, target, wide_count)
        picks = jnp.full((wide_count,), tile_dev, jnp.int32).at[chunk_index].set(
            jnp.arange(tile_dev, dtype=jnp.int32), mode="drop"
        )
        outgoing = jnp.take(tiles, picks, axis=0, mode="clip")
        arrived = lax.all_to_all(outgoing, "wide", split_axis=0, concat_axis=0, tiled=True)
        summed = add_products(arrived, arrived_labels[:, rank, :], panel_tiles, summed)
    summed = ring_sum(summed, lax.axis_size("grp"))
    return summed.reshape(out_dev * tile_side, gathered.shape[1])


def solution(mesh):
    return jax.shard_map(
        per_device,
        mesh=mesh,
        in_specs=(
            P(("grp", "wide"), None, None),
            P(("grp", "wide")),
            P(("grp", "wide")),
            P(),
            P("grp", None),
        ),
        out_specs=P("wide", None),
        check_vma=False,
    )
```

```python
import functools

import jax
import jax.numpy as jnp
from jax import lax
from jax.experimental import pallas as pl
from jax.experimental.pallas import tpu as pltpu
from jax.sharding import PartitionSpec as P


MESH = pl.DeviceIdType.MESH


def ring_sum_kernel(n, x_ref, out_ref, sbuf, rbuf, send_sem, recv_sem):
    me = lax.axis_index("grp")
    column = lax.axis_index("wide")
    right = lax.rem(me + 1, n)
    left = lax.rem(me + n - 1, n)
    half = x_ref.shape[1] // 2
    neighbours = (right, left)

    barrier = pltpu.get_barrier_semaphore()
    for neighbour in (left, right):
        pl.semaphore_signal(barrier, inc=1, device_id=(neighbour, column), device_id_type=MESH)
    pl.semaphore_wait(barrier, 2)

    def send(way, step, src, dst):
        copy = pltpu.make_async_remote_copy(
            src_ref=src,
            dst_ref=dst,
            send_sem=send_sem.at[way, step],
            recv_sem=recv_sem.at[way, step],
            device_id=(neighbours[way], column),
            device_id_type=MESH,
        )
        copy.start()
        return copy

    for step in range(n - 1):
        copies = []
        for way in range(2):
            sign = 1 - 2 * way
            rows = pl.ds(way * half, half)
            chunk = lax.rem(me - sign * (step + 1) + 2 * n, n)
            if step == 0:
                src = x_ref.at[chunk, rows]
            else:
                sbuf[way, step] = rbuf[way, step - 1] + x_ref[chunk, rows]
                src = sbuf.at[way, step]
            copies.append(send(way, step, src, rbuf.at[way, step]))
        for copy in copies:
            copy.wait()

    for way in range(2):
        rows = pl.ds(way * half, half)
        out_ref[me, rows] = rbuf[way, n - 2] + x_ref[me, rows]

    for step in range(n - 1):
        copies = []
        for way in range(2):
            sign = 1 - 2 * way
            rows = pl.ds(way * half, half)
            chunk = lax.rem(me - sign * step + 2 * n, n)
            copies.append(send(way, n - 1 + step, out_ref.at[chunk, rows], out_ref.at[chunk, rows]))
        for copy in copies:
            copy.wait()


def ring_sum(x, n, ident):
    half = x.shape[1] // 2
    return pl.pallas_call(
        functools.partial(ring_sum_kernel, n),
        out_shape=jax.ShapeDtypeStruct(x.shape, x.dtype),
        in_specs=[pl.BlockSpec(memory_space=pltpu.VMEM)],
        out_specs=pl.BlockSpec(memory_space=pltpu.VMEM),
        scratch_shapes=[
            pltpu.VMEM((2, n - 1, half, x.shape[2]), x.dtype),
            pltpu.VMEM((2, n - 1, half, x.shape[2]), x.dtype),
            pltpu.SemaphoreType.DMA((2, 2 * (n - 1))),
            pltpu.SemaphoreType.DMA((2, 2 * (n - 1))),
        ],
        compiler_params=pltpu.CompilerParams(
            collective_id=ident, has_side_effects=True, vmem_limit_bytes=48 * 1024 * 1024
        ),
    )(x)


def place_slots(row_ids, owner_map, out_dev):
    table_ids = jnp.arange(owner_map.shape[0], dtype=jnp.int32)
    position = jnp.sum(jnp.where(row_ids[..., None] == table_ids, owner_map, 0), axis=-1)
    target = position // out_dev
    serial = jnp.arange(row_ids.shape[-1], dtype=jnp.int32)
    earlier = (target[..., :, None] == target[..., None, :]) & (serial[:, None] > serial[None, :])
    ranking = jnp.sum(earlier.astype(jnp.int32), axis=-1)
    return (position % out_dev, target, ranking)


def products_kernel(count_ref, order_ref, rows_ref, ks_ref, arrived_ref, panel_ref, init_ref, out_ref):
    out_ref[...] = init_ref[...]
    columns = panel_ref.shape[2]
    side = arrived_ref.shape[2]

    def body(i, carry):
        source = order_ref[i]
        row = rows_ref[source]
        k = ks_ref[source]
        tile = arrived_ref[source]
        for c in range(columns // side):
            cols = pl.ds(c * side, side)
            out_ref[row, :, cols] += jnp.dot(
                tile, panel_ref[k, :, cols], preferred_element_type=jnp.float32
            )
        return carry

    lax.fori_loop(0, count_ref[0], body, 0)


def slot_order(arrived_labels, out_dev):
    rows = arrived_labels[:, 0]
    ks = arrived_labels[:, 1]
    vacant = (rows >= out_dev).astype(jnp.int32)
    order = jnp.argsort(vacant, stable=True).astype(jnp.int32)
    count = jnp.reshape(rows.shape[0] - jnp.sum(vacant), (1,)).astype(jnp.int32)
    return count, order, rows, ks


def add_products(arrived, schedule, panel_tiles, running):
    vmem = pl.BlockSpec(memory_space=pltpu.VMEM)
    smem = pl.BlockSpec(memory_space=pltpu.SMEM)
    return pl.pallas_call(
        products_kernel,
        out_shape=jax.ShapeDtypeStruct(running.shape, jnp.float32),
        in_specs=[smem, smem, smem, smem, vmem, vmem, vmem],
        out_specs=vmem,
        compiler_params=pltpu.CompilerParams(vmem_limit_bytes=48 * 1024 * 1024),
    )(*schedule, arrived, panel_tiles, running)


def per_device(tiles, contraction, row_tile, owner_map, panel):
    wide_count = lax.axis_size("wide")
    tile_dev = tiles.shape[0]
    tile_side = tiles.shape[1]
    out_dev = owner_map.shape[0] // wide_count
    most_slots = tile_dev * 8 // (3 * wide_count)
    slot_total = wide_count * most_slots
    local_row, target, ranking = place_slots(row_tile, owner_map, out_dev)
    slot_index = target * most_slots + ranking
    vacant_label = jnp.stack(
        [jnp.full((slot_total,), out_dev, jnp.int32), jnp.zeros((slot_total,), jnp.int32)], axis=1
    )
    label_out = vacant_label.at[slot_index].set(jnp.stack([local_row, contraction], axis=1))
    arrived_labels = lax.all_to_all(label_out, "wide", split_axis=0, concat_axis=0, tiled=True)
    arrived_labels = arrived_labels.reshape(wide_count, most_slots, 2)
    gathered = lax.all_gather(panel, "grp", axis=0, tiled=True)
    panel_tiles = gathered.reshape(gathered.shape[0] // tile_side, tile_side, gathered.shape[1])
    band = tile_side // 2
    arrived_labels = arrived_labels.reshape(wide_count, most_slots, 2)
    schedules = [slot_order(arrived_labels[:, rank, :], out_dev) for rank in range(most_slots)]
    outgoing = {}
    for rank in range(most_slots):
        chunk_index = jnp.where(ranking == rank, target, wide_count)
        picks = jnp.full((wide_count,), tile_dev, jnp.int32).at[chunk_index].set(
            jnp.arange(tile_dev, dtype=jnp.int32), mode="drop"
        )
        for half in range(2):
            rows = tiles[:, half * band:(half + 1) * band, :]
            outgoing[rank, half] = jnp.take(rows, picks, axis=0, mode="clip")

    def exchange(block):
        return lax.all_to_all(block, "wide", split_axis=0, concat_axis=0, tiled=True)

    zero = jnp.zeros((out_dev, band, gathered.shape[1]), jnp.float32)
    upper = add_products(exchange(outgoing[0, 0]), schedules[0], panel_tiles, zero)
    lower = add_products(exchange(outgoing[0, 1]), schedules[0], panel_tiles, zero)
    late, upper = lax.optimization_barrier((outgoing[1, 0], upper))
    upper = add_products(exchange(late), schedules[1], panel_tiles, upper)
    late, lower = lax.optimization_barrier((outgoing[1, 1], lower))
    arrived = exchange(late)
    upper = ring_sum(upper, lax.axis_size("grp"), 0)
    lower = add_products(arrived, schedules[1], panel_tiles, lower)
    lower = ring_sum(lower, lax.axis_size("grp"), 1)
    summed = jnp.concatenate([upper, lower], axis=1)
    return summed.reshape(out_dev * tile_side, gathered.shape[1])


def solution(mesh):
    return jax.shard_map(
        per_device,
        mesh=mesh,
        in_specs=(
            P(("grp", "wide"), None, None),
            P(("grp", "wide")),
            P(("grp", "wide")),
            P(),
            P("grp", None),
        ),
        out_specs=P("wide", None),
        check_vma=False,
    )
```

```python
import functools

import jax
import jax.numpy as jnp
from jax import lax
from jax.experimental import pallas as pl
from jax.experimental.pallas import tpu as pltpu
from jax.sharding import PartitionSpec as P


MESH = pl.DeviceIdType.MESH


def ring_sum_kernel(n, x_ref, out_ref, sbuf, rbuf, send_sem, recv_sem):
    me = lax.axis_index("grp")
    column = lax.axis_index("wide")
    right = lax.rem(me + 1, n)
    left = lax.rem(me + n - 1, n)
    half = x_ref.shape[1] // 2
    neighbours = (right, left)

    barrier = pltpu.get_barrier_semaphore()
    for neighbour in (left, right):
        pl.semaphore_signal(barrier, inc=1, device_id=(neighbour, column), device_id_type=MESH)
    pl.semaphore_wait(barrier, 2)

    def send(way, step, src, dst):
        copy = pltpu.make_async_remote_copy(
            src_ref=src,
            dst_ref=dst,
            send_sem=send_sem.at[way, step],
            recv_sem=recv_sem.at[way, step],
            device_id=(neighbours[way], column),
            device_id_type=MESH,
        )
        copy.start()
        return copy

    for step in range(n - 1):
        copies = []
        for way in range(2):
            sign = 1 - 2 * way
            rows = pl.ds(way * half, half)
            chunk = lax.rem(me - sign * (step + 1) + 2 * n, n)
            if step == 0:
                src = x_ref.at[chunk, rows]
            else:
                sbuf[way, step] = rbuf[way, step - 1] + x_ref[chunk, rows]
                src = sbuf.at[way, step]
            copies.append(send(way, step, src, rbuf.at[way, step]))
        for copy in copies:
            copy.wait()

    for way in range(2):
        rows = pl.ds(way * half, half)
        out_ref[me, rows] = rbuf[way, n - 2] + x_ref[me, rows]

    for step in range(n - 1):
        copies = []
        for way in range(2):
            sign = 1 - 2 * way
            rows = pl.ds(way * half, half)
            chunk = lax.rem(me - sign * step + 2 * n, n)
            copies.append(send(way, n - 1 + step, out_ref.at[chunk, rows], out_ref.at[chunk, rows]))
        for copy in copies:
            copy.wait()


def ring_sum(x, n, ident):
    half = x.shape[1] // 2
    return pl.pallas_call(
        functools.partial(ring_sum_kernel, n),
        out_shape=jax.ShapeDtypeStruct(x.shape, x.dtype),
        in_specs=[pl.BlockSpec(memory_space=pltpu.VMEM)],
        out_specs=pl.BlockSpec(memory_space=pltpu.VMEM),
        scratch_shapes=[
            pltpu.VMEM((2, n - 1, half, x.shape[2]), x.dtype),
            pltpu.VMEM((2, n - 1, half, x.shape[2]), x.dtype),
            pltpu.SemaphoreType.DMA((2, 2 * (n - 1))),
            pltpu.SemaphoreType.DMA((2, 2 * (n - 1))),
        ],
        compiler_params=pltpu.CompilerParams(
            collective_id=ident, has_side_effects=True, vmem_limit_bytes=48 * 1024 * 1024
        ),
    )(x)


def place_slots(row_ids, owner_map, out_dev):
    table_ids = jnp.arange(owner_map.shape[0], dtype=jnp.int32)
    position = jnp.sum(jnp.where(row_ids[..., None] == table_ids, owner_map, 0), axis=-1)
    target = position // out_dev
    serial = jnp.arange(row_ids.shape[-1], dtype=jnp.int32)
    earlier = (target[..., :, None] == target[..., None, :]) & (serial[:, None] > serial[None, :])
    ranking = jnp.sum(earlier.astype(jnp.int32), axis=-1)
    return (position % out_dev, target, ranking)


def products_kernel(count_ref, order_ref, rows_ref, ks_ref, arrived_ref, panel_ref, init_ref, out_ref):
    out_ref[...] = init_ref[...]
    columns = panel_ref.shape[2]
    side = arrived_ref.shape[2]

    def body(i, carry):
        source = order_ref[i]
        row = rows_ref[source]
        k = ks_ref[source]
        tile = arrived_ref[source]
        for c in range(columns // side):
            cols = pl.ds(c * side, side)
            out_ref[row, :, cols] += jnp.dot(
                tile, panel_ref[k, :, cols], preferred_element_type=jnp.float32
            )
        return carry

    lax.fori_loop(0, count_ref[0], body, 0)


def slot_order(arrived_labels, out_dev):
    rows = arrived_labels[:, 0]
    ks = arrived_labels[:, 1]
    vacant = (rows >= out_dev).astype(jnp.int32)
    order = jnp.argsort(vacant, stable=True).astype(jnp.int32)
    count = jnp.reshape(rows.shape[0] - jnp.sum(vacant), (1,)).astype(jnp.int32)
    return count, order, rows, ks


def add_products(arrived, schedule, panel_tiles, running):
    vmem = pl.BlockSpec(memory_space=pltpu.VMEM)
    smem = pl.BlockSpec(memory_space=pltpu.SMEM)
    return pl.pallas_call(
        products_kernel,
        out_shape=jax.ShapeDtypeStruct(running.shape, jnp.float32),
        in_specs=[smem, smem, smem, smem, vmem, vmem, vmem],
        out_specs=vmem,
        compiler_params=pltpu.CompilerParams(vmem_limit_bytes=48 * 1024 * 1024),
    )(*schedule, arrived, panel_tiles, running)


def per_device(tiles, contraction, row_tile, owner_map, panel):
    wide_count = lax.axis_size("wide")
    tile_dev = tiles.shape[0]
    tile_side = tiles.shape[1]
    out_dev = owner_map.shape[0] // wide_count
    most_slots = tile_dev * 8 // (3 * wide_count)
    slot_total = wide_count * most_slots
    local_row, target, ranking = place_slots(row_tile, owner_map, out_dev)
    slot_index = target * most_slots + ranking
    vacant_label = jnp.stack(
        [jnp.full((slot_total,), out_dev, jnp.int32), jnp.zeros((slot_total,), jnp.int32)], axis=1
    )
    label_out = vacant_label.at[slot_index].set(jnp.stack([local_row, contraction], axis=1))
    arrived_labels = lax.all_to_all(label_out, "wide", split_axis=0, concat_axis=0, tiled=True)
    arrived_labels = arrived_labels.reshape(wide_count, most_slots, 2)
    gathered = lax.all_gather(panel, "grp", axis=0, tiled=True)
    panel_tiles = gathered.reshape(gathered.shape[0] // tile_side, tile_side, gathered.shape[1])
    band = tile_side * 3 // 4
    arrived_labels = arrived_labels.reshape(wide_count, most_slots, 2)
    schedules = [slot_order(arrived_labels[:, rank, :], out_dev) for rank in range(most_slots)]
    picks = []
    for rank in range(most_slots):
        chunk_index = jnp.where(ranking == rank, target, wide_count)
        picks.append(jnp.full((wide_count,), tile_dev, jnp.int32).at[chunk_index].set(
            jnp.arange(tile_dev, dtype=jnp.int32), mode="drop"
        ))
    first = jnp.take(tiles, picks[0], axis=0, mode="clip")
    upper_out = jnp.take(tiles[:, :band, :], picks[1], axis=0, mode="clip")
    lower_out = jnp.take(tiles[:, band:, :], picks[1], axis=0, mode="clip")

    def exchange(block):
        return lax.all_to_all(block, "wide", split_axis=0, concat_axis=0, tiled=True)

    zero = jnp.zeros((out_dev, tile_side, gathered.shape[1]), jnp.float32)
    whole = add_products(exchange(first), schedules[0], panel_tiles, zero)
    upper = add_products(exchange(upper_out), schedules[1], panel_tiles, whole[:, :band, :])
    lower_out, whole = lax.optimization_barrier((lower_out, whole))
    arrived = exchange(lower_out)
    upper = ring_sum(upper, lax.axis_size("grp"), 0)
    lower = add_products(arrived, schedules[1], panel_tiles, whole[:, band:, :])
    lower = ring_sum(lower, lax.axis_size("grp"), 1)
    summed = jnp.concatenate([upper, lower], axis=1)
    return summed.reshape(out_dev * tile_side, gathered.shape[1])


def solution(mesh):
    return jax.shard_map(
        per_device,
        mesh=mesh,
        in_specs=(
            P(("grp", "wide"), None, None),
            P(("grp", "wide")),
            P(("grp", "wide")),
            P(),
            P("grp", None),
        ),
        out_specs=P("wide", None),
        check_vma=False,
    )
```

```python
import functools

import jax
import jax.numpy as jnp
from jax import lax
from jax.experimental import pallas as pl
from jax.experimental.pallas import tpu as pltpu
from jax.sharding import PartitionSpec as P


MESH = pl.DeviceIdType.MESH


def ring_sum_kernel(n, x_ref, out_ref, sbuf, rbuf, send_sem, recv_sem):
    me = lax.axis_index("grp")
    column = lax.axis_index("wide")
    right = lax.rem(me + 1, n)
    left = lax.rem(me + n - 1, n)
    half = x_ref.shape[1] // 2
    neighbours = (right, left)

    barrier = pltpu.get_barrier_semaphore()
    for neighbour in (left, right):
        pl.semaphore_signal(barrier, inc=1, device_id=(neighbour, column), device_id_type=MESH)
    pl.semaphore_wait(barrier, 2)

    def send(way, step, src, dst):
        copy = pltpu.make_async_remote_copy(
            src_ref=src,
            dst_ref=dst,
            send_sem=send_sem.at[way, step],
            recv_sem=recv_sem.at[way, step],
            device_id=(neighbours[way], column),
            device_id_type=MESH,
        )
        copy.start()
        return copy

    for step in range(n - 1):
        copies = []
        for way in range(2):
            sign = 1 - 2 * way
            rows = pl.ds(way * half, half)
            chunk = lax.rem(me - sign * (step + 1) + 2 * n, n)
            if step == 0:
                src = x_ref.at[chunk, rows]
            else:
                sbuf[way, step] = rbuf[way, step - 1] + x_ref[chunk, rows]
                src = sbuf.at[way, step]
            copies.append(send(way, step, src, rbuf.at[way, step]))
        for copy in copies:
            copy.wait()

    for way in range(2):
        rows = pl.ds(way * half, half)
        out_ref[me, rows] = rbuf[way, n - 2] + x_ref[me, rows]

    for step in range(n - 1):
        copies = []
        for way in range(2):
            sign = 1 - 2 * way
            rows = pl.ds(way * half, half)
            chunk = lax.rem(me - sign * step + 2 * n, n)
            copies.append(send(way, n - 1 + step, out_ref.at[chunk, rows], out_ref.at[chunk, rows]))
        for copy in copies:
            copy.wait()


def ring_sum(x, n, ident):
    half = x.shape[1] // 2
    return pl.pallas_call(
        functools.partial(ring_sum_kernel, n),
        out_shape=jax.ShapeDtypeStruct(x.shape, x.dtype),
        in_specs=[pl.BlockSpec(memory_space=pltpu.VMEM)],
        out_specs=pl.BlockSpec(memory_space=pltpu.VMEM),
        scratch_shapes=[
            pltpu.VMEM((2, n - 1, half, x.shape[2]), x.dtype),
            pltpu.VMEM((2, n - 1, half, x.shape[2]), x.dtype),
            pltpu.SemaphoreType.DMA((2, 2 * (n - 1))),
            pltpu.SemaphoreType.DMA((2, 2 * (n - 1))),
        ],
        compiler_params=pltpu.CompilerParams(
            collective_id=ident, has_side_effects=True, vmem_limit_bytes=48 * 1024 * 1024
        ),
    )(x)


def place_slots(row_ids, owner_map, out_dev):
    table_ids = jnp.arange(owner_map.shape[0], dtype=jnp.int32)
    position = jnp.sum(jnp.where(row_ids[..., None] == table_ids, owner_map, 0), axis=-1)
    target = position // out_dev
    serial = jnp.arange(row_ids.shape[-1], dtype=jnp.int32)
    earlier = (target[..., :, None] == target[..., None, :]) & (serial[:, None] > serial[None, :])
    ranking = jnp.sum(earlier.astype(jnp.int32), axis=-1)
    return (position % out_dev, target, ranking)


def products_kernel(count_ref, order_ref, rows_ref, ks_ref, arrived_ref, panel_ref, init_ref, out_ref):
    out_ref[...] = init_ref[...]
    columns = panel_ref.shape[2]
    side = arrived_ref.shape[2]

    def body(i, carry):
        source = order_ref[i]
        row = rows_ref[source]
        k = ks_ref[source]
        tile = arrived_ref[source]
        for c in range(columns // side):
            cols = pl.ds(c * side, side)
            out_ref[row, :, cols] += jnp.dot(
                tile, panel_ref[k, :, cols], preferred_element_type=jnp.float32
            )
        return carry

    lax.fori_loop(0, count_ref[0], body, 0)


def slot_order(arrived_labels, out_dev):
    rows = arrived_labels[:, 0]
    ks = arrived_labels[:, 1]
    vacant = (rows >= out_dev).astype(jnp.int32)
    order = jnp.argsort(vacant, stable=True).astype(jnp.int32)
    count = jnp.reshape(rows.shape[0] - jnp.sum(vacant), (1,)).astype(jnp.int32)
    return count, order, rows, ks


def add_products(arrived, schedule, panel_tiles, running):
    vmem = pl.BlockSpec(memory_space=pltpu.VMEM)
    smem = pl.BlockSpec(memory_space=pltpu.SMEM)
    return pl.pallas_call(
        products_kernel,
        out_shape=jax.ShapeDtypeStruct(running.shape, jnp.float32),
        in_specs=[smem, smem, smem, smem, vmem, vmem, vmem],
        out_specs=vmem,
        compiler_params=pltpu.CompilerParams(vmem_limit_bytes=48 * 1024 * 1024),
    )(*schedule, arrived, panel_tiles, running)


def per_device(tiles, contraction, row_tile, owner_map, panel):
    wide_count = lax.axis_size("wide")
    tile_dev = tiles.shape[0]
    tile_side = tiles.shape[1]
    out_dev = owner_map.shape[0] // wide_count
    most_slots = tile_dev * 8 // (3 * wide_count)
    slot_total = wide_count * most_slots
    local_row, target, ranking = place_slots(row_tile, owner_map, out_dev)
    slot_index = target * most_slots + ranking
    vacant_label = jnp.stack(
        [jnp.full((slot_total,), out_dev, jnp.int32), jnp.zeros((slot_total,), jnp.int32)], axis=1
    )
    label_out = vacant_label.at[slot_index].set(jnp.stack([local_row, contraction], axis=1))
    arrived_labels = lax.all_to_all(label_out, "wide", split_axis=0, concat_axis=0, tiled=True)
    arrived_labels = arrived_labels.reshape(wide_count, most_slots, 2)
    gathered = lax.all_gather(panel, "grp", axis=0, tiled=True)
    panel_tiles = gathered.reshape(gathered.shape[0] // tile_side, tile_side, gathered.shape[1])
    band = tile_side * 5 // 8
    arrived_labels = arrived_labels.reshape(wide_count, most_slots, 2)
    schedules = [slot_order(arrived_labels[:, rank, :], out_dev) for rank in range(most_slots)]
    picks = []
    for rank in range(most_slots):
        chunk_index = jnp.where(ranking == rank, target, wide_count)
        picks.append(jnp.full((wide_count,), tile_dev, jnp.int32).at[chunk_index].set(
            jnp.arange(tile_dev, dtype=jnp.int32), mode="drop"
        ))
    first = jnp.take(tiles, picks[0], axis=0, mode="clip")
    upper_out = jnp.take(tiles[:, :band, :], picks[1], axis=0, mode="clip")
    lower_out = jnp.take(tiles[:, band:, :], picks[1], axis=0, mode="clip")

    def exchange(block):
        return lax.all_to_all(block, "wide", split_axis=0, concat_axis=0, tiled=True)

    zero = jnp.zeros((out_dev, tile_side, gathered.shape[1]), jnp.float32)
    whole = add_products(exchange(first), schedules[0], panel_tiles, zero)
    upper = add_products(exchange(upper_out), schedules[1], panel_tiles, whole[:, :band, :])
    lower_out, whole = lax.optimization_barrier((lower_out, whole))
    arrived = exchange(lower_out)
    upper = ring_sum(upper, lax.axis_size("grp"), 0)
    lower = add_products(arrived, schedules[1], panel_tiles, whole[:, band:, :])
    lower = ring_sum(lower, lax.axis_size("grp"), 1)
    summed = jnp.concatenate([upper, lower], axis=1)
    return summed.reshape(out_dev * tile_side, gathered.shape[1])


def solution(mesh):
    return jax.shard_map(
        per_device,
        mesh=mesh,
        in_specs=(
            P(("grp", "wide"), None, None),
            P(("grp", "wide")),
            P(("grp", "wide")),
            P(),
            P("grp", None),
        ),
        out_specs=P("wide", None),
        check_vma=False,
    )
```

```python
import functools

import jax
import jax.numpy as jnp
from jax import lax
from jax.experimental import pallas as pl
from jax.experimental.pallas import tpu as pltpu
from jax.sharding import PartitionSpec as P


MESH = pl.DeviceIdType.MESH


def ring_sum_kernel(n, x_ref, out_ref, sbuf, rbuf, send_sem, recv_sem):
    me = lax.axis_index("grp")
    column = lax.axis_index("wide")
    right = lax.rem(me + 1, n)
    left = lax.rem(me + n - 1, n)
    half = x_ref.shape[1] // 2
    neighbours = (right, left)

    barrier = pltpu.get_barrier_semaphore()
    for neighbour in (left, right):
        pl.semaphore_signal(barrier, inc=1, device_id=(neighbour, column), device_id_type=MESH)
    pl.semaphore_wait(barrier, 2)

    def send(way, step, src, dst):
        copy = pltpu.make_async_remote_copy(
            src_ref=src,
            dst_ref=dst,
            send_sem=send_sem.at[way, step],
            recv_sem=recv_sem.at[way, step],
            device_id=(neighbours[way], column),
            device_id_type=MESH,
        )
        copy.start()
        return copy

    for step in range(n - 1):
        copies = []
        for way in range(2):
            sign = 1 - 2 * way
            rows = pl.ds(way * half, half)
            chunk = lax.rem(me - sign * (step + 1) + 2 * n, n)
            if step == 0:
                src = x_ref.at[chunk, rows]
            else:
                sbuf[way, step] = rbuf[way, step - 1] + x_ref[chunk, rows]
                src = sbuf.at[way, step]
            copies.append(send(way, step, src, rbuf.at[way, step]))
        for copy in copies:
            copy.wait()

    for way in range(2):
        rows = pl.ds(way * half, half)
        out_ref[me, rows] = rbuf[way, n - 2] + x_ref[me, rows]

    for step in range(n - 1):
        copies = []
        for way in range(2):
            sign = 1 - 2 * way
            rows = pl.ds(way * half, half)
            chunk = lax.rem(me - sign * step + 2 * n, n)
            copies.append(send(way, n - 1 + step, out_ref.at[chunk, rows], out_ref.at[chunk, rows]))
        for copy in copies:
            copy.wait()


def ring_sum(x, n, ident):
    half = x.shape[1] // 2
    return pl.pallas_call(
        functools.partial(ring_sum_kernel, n),
        out_shape=jax.ShapeDtypeStruct(x.shape, x.dtype),
        in_specs=[pl.BlockSpec(memory_space=pltpu.VMEM)],
        out_specs=pl.BlockSpec(memory_space=pltpu.VMEM),
        scratch_shapes=[
            pltpu.VMEM((2, n - 1, half, x.shape[2]), x.dtype),
            pltpu.VMEM((2, n - 1, half, x.shape[2]), x.dtype),
            pltpu.SemaphoreType.DMA((2, 2 * (n - 1))),
            pltpu.SemaphoreType.DMA((2, 2 * (n - 1))),
        ],
        compiler_params=pltpu.CompilerParams(
            collective_id=ident, has_side_effects=True, vmem_limit_bytes=48 * 1024 * 1024
        ),
    )(x)


def place_slots(row_ids, owner_map, out_dev):
    table_ids = jnp.arange(owner_map.shape[0], dtype=jnp.int32)
    position = jnp.sum(jnp.where(row_ids[..., None] == table_ids, owner_map, 0), axis=-1)
    target = position // out_dev
    serial = jnp.arange(row_ids.shape[-1], dtype=jnp.int32)
    earlier = (target[..., :, None] == target[..., None, :]) & (serial[:, None] > serial[None, :])
    ranking = jnp.sum(earlier.astype(jnp.int32), axis=-1)
    return (position % out_dev, target, ranking)


def products_kernel(count_ref, order_ref, rows_ref, ks_ref, arrived_ref, panel_ref, init_ref, out_ref):
    out_ref[...] = init_ref[...]
    columns = panel_ref.shape[2]
    side = arrived_ref.shape[2]

    def body(i, carry):
        source = order_ref[i]
        row = rows_ref[source]
        k = ks_ref[source]
        tile = arrived_ref[source]
        for c in range(columns // side):
            cols = pl.ds(c * side, side)
            out_ref[row, :, cols] += jnp.dot(
                tile, panel_ref[k, :, cols], preferred_element_type=jnp.float32
            )
        return carry

    lax.fori_loop(0, count_ref[0], body, 0)


def slot_order(arrived_labels, out_dev):
    rows = arrived_labels[:, 0]
    ks = arrived_labels[:, 1]
    vacant = (rows >= out_dev).astype(jnp.int32)
    order = jnp.argsort(vacant, stable=True).astype(jnp.int32)
    count = jnp.reshape(rows.shape[0] - jnp.sum(vacant), (1,)).astype(jnp.int32)
    return count, order, rows, ks


def add_products(arrived, schedule, panel_tiles, running):
    vmem = pl.BlockSpec(memory_space=pltpu.VMEM)
    smem = pl.BlockSpec(memory_space=pltpu.SMEM)
    return pl.pallas_call(
        products_kernel,
        out_shape=jax.ShapeDtypeStruct(running.shape, jnp.float32),
        in_specs=[smem, smem, smem, smem, vmem, vmem, vmem],
        out_specs=vmem,
        compiler_params=pltpu.CompilerParams(vmem_limit_bytes=48 * 1024 * 1024),
    )(*schedule, arrived, panel_tiles, running)


def per_device(tiles, contraction, row_tile, owner_map, panel):
    wide_count = lax.axis_size("wide")
    tile_dev = tiles.shape[0]
    tile_side = tiles.shape[1]
    out_dev = owner_map.shape[0] // wide_count
    most_slots = tile_dev * 8 // (3 * wide_count)
    slot_total = wide_count * most_slots
    local_row, target, ranking = place_slots(row_tile, owner_map, out_dev)
    slot_index = target * most_slots + ranking
    vacant_label = jnp.stack(
        [jnp.full((slot_total,), out_dev, jnp.int32), jnp.zeros((slot_total,), jnp.int32)], axis=1
    )
    label_out = vacant_label.at[slot_index].set(jnp.stack([local_row, contraction], axis=1))
    arrived_labels = lax.all_to_all(label_out, "wide", split_axis=0, concat_axis=0, tiled=True)
    arrived_labels = arrived_labels.reshape(wide_count, most_slots, 2)
    grp_count = lax.axis_size("grp")
    pieces = [panel] + [
        lax.ppermute(panel, "grp", [(j, (j + shift) % grp_count) for j in range(grp_count)])
        for shift in range(1, grp_count)
    ]
    gathered = jnp.concatenate(pieces, axis=0)
    panel_tiles = gathered.reshape(gathered.shape[0] // tile_side, tile_side, gathered.shape[1])
    held = panel.shape[0] // tile_side
    owner = arrived_labels[..., 1] // held
    shift = lax.rem(lax.axis_index("grp") - owner + grp_count, grp_count)
    arrived_labels = arrived_labels.at[..., 1].set(shift * held + arrived_labels[..., 1] % held)
    band = tile_side * 5 // 8
    arrived_labels = arrived_labels.reshape(wide_count, most_slots, 2)
    schedules = [slot_order(arrived_labels[:, rank, :], out_dev) for rank in range(most_slots)]
    picks = []
    for rank in range(most_slots):
        chunk_index = jnp.where(ranking == rank, target, wide_count)
        picks.append(jnp.full((wide_count,), tile_dev, jnp.int32).at[chunk_index].set(
            jnp.arange(tile_dev, dtype=jnp.int32), mode="drop"
        ))
    first = jnp.take(tiles, picks[0], axis=0, mode="clip")
    upper_out = jnp.take(tiles[:, :band, :], picks[1], axis=0, mode="clip")
    lower_out = jnp.take(tiles[:, band:, :], picks[1], axis=0, mode="clip")

    def exchange(block):
        return lax.all_to_all(block, "wide", split_axis=0, concat_axis=0, tiled=True)

    zero = jnp.zeros((out_dev, tile_side, gathered.shape[1]), jnp.float32)
    whole = add_products(exchange(first), schedules[0], panel_tiles, zero)
    upper = add_products(exchange(upper_out), schedules[1], panel_tiles, whole[:, :band, :])
    lower_out, whole = lax.optimization_barrier((lower_out, whole))
    arrived = exchange(lower_out)
    upper = ring_sum(upper, lax.axis_size("grp"), 0)
    lower = add_products(arrived, schedules[1], panel_tiles, whole[:, band:, :])
    lower = ring_sum(lower, lax.axis_size("grp"), 1)
    summed = jnp.concatenate([upper, lower], axis=1)
    return summed.reshape(out_dev * tile_side, gathered.shape[1])


def solution(mesh):
    return jax.shard_map(
        per_device,
        mesh=mesh,
        in_specs=(
            P(("grp", "wide"), None, None),
            P(("grp", "wide")),
            P(("grp", "wide")),
            P(),
            P("grp", None),
        ),
        out_specs=P("wide", None),
        check_vma=False,
    )
```

```python
import functools

import jax
import jax.numpy as jnp
from jax import lax
from jax.experimental import pallas as pl
from jax.experimental.pallas import tpu as pltpu
from jax.sharding import PartitionSpec as P


MESH = pl.DeviceIdType.MESH


def ring_sum_kernel(n, x_ref, out_ref, sbuf, rbuf, send_sem, recv_sem):
    me = lax.axis_index("grp")
    column = lax.axis_index("wide")
    right = lax.rem(me + 1, n)
    left = lax.rem(me + n - 1, n)
    half = x_ref.shape[1] // 2
    neighbours = (right, left)

    barrier = pltpu.get_barrier_semaphore()
    for neighbour in (left, right):
        pl.semaphore_signal(barrier, inc=1, device_id=(neighbour, column), device_id_type=MESH)
    pl.semaphore_wait(barrier, 2)

    def send(way, step, src, dst):
        copy = pltpu.make_async_remote_copy(
            src_ref=src,
            dst_ref=dst,
            send_sem=send_sem.at[way, step],
            recv_sem=recv_sem.at[way, step],
            device_id=(neighbours[way], column),
            device_id_type=MESH,
        )
        copy.start()
        return copy

    for step in range(n - 1):
        copies = []
        for way in range(2):
            sign = 1 - 2 * way
            rows = pl.ds(way * half, half)
            chunk = lax.rem(me - sign * (step + 1) + 2 * n, n)
            if step == 0:
                src = x_ref.at[chunk, rows]
            else:
                sbuf[way, step] = rbuf[way, step - 1] + x_ref[chunk, rows]
                src = sbuf.at[way, step]
            copies.append(send(way, step, src, rbuf.at[way, step]))
        for copy in copies:
            copy.wait()

    for way in range(2):
        rows = pl.ds(way * half, half)
        out_ref[me, rows] = rbuf[way, n - 2] + x_ref[me, rows]

    for step in range(n - 1):
        copies = []
        for way in range(2):
            sign = 1 - 2 * way
            rows = pl.ds(way * half, half)
            chunk = lax.rem(me - sign * step + 2 * n, n)
            copies.append(send(way, n - 1 + step, out_ref.at[chunk, rows], out_ref.at[chunk, rows]))
        for copy in copies:
            copy.wait()


def ring_sum(x, n, ident):
    half = x.shape[1] // 2
    return pl.pallas_call(
        functools.partial(ring_sum_kernel, n),
        out_shape=jax.ShapeDtypeStruct(x.shape, x.dtype),
        in_specs=[pl.BlockSpec(memory_space=pltpu.VMEM)],
        out_specs=pl.BlockSpec(memory_space=pltpu.VMEM),
        scratch_shapes=[
            pltpu.VMEM((2, n - 1, half, x.shape[2]), x.dtype),
            pltpu.VMEM((2, n - 1, half, x.shape[2]), x.dtype),
            pltpu.SemaphoreType.DMA((2, 2 * (n - 1))),
            pltpu.SemaphoreType.DMA((2, 2 * (n - 1))),
        ],
        compiler_params=pltpu.CompilerParams(
            collective_id=ident, has_side_effects=True, vmem_limit_bytes=48 * 1024 * 1024
        ),
    )(x)


def label_kernel(n, lab_ref, out_ref, send_sem, recv_sem):
    me = lax.axis_index("wide")
    row = lax.axis_index("grp")
    barrier = pltpu.get_barrier_semaphore()

    def greet(shift, carry):
        peer = lax.rem(me + shift, n)
        pl.semaphore_signal(barrier, inc=1, device_id=(row, peer), device_id_type=MESH)
        return carry

    lax.fori_loop(1, n, greet, 0)
    pl.semaphore_wait(barrier, n - 1)
    out_ref[me] = lab_ref[me]

    def link(source, target, peer):
        return pltpu.make_async_remote_copy(
            src_ref=lab_ref.at[target],
            dst_ref=out_ref.at[source],
            send_sem=send_sem.at[target],
            recv_sem=recv_sem.at[source],
            device_id=(row, peer),
            device_id_type=MESH,
        )

    def start(shift, carry):
        peer = lax.rem(me + shift, n)
        link(me, peer, peer).start()
        return carry

    lax.fori_loop(1, n, start, 0)

    def finish(shift, carry):
        peer = lax.rem(me + shift, n)
        link(me, peer, peer).wait_send()
        source = lax.rem(me + n - shift, n)
        link(source, source, source).wait_recv()
        return carry

    lax.fori_loop(1, n, finish, 0)


def swap_labels(lab, n):
    return pl.pallas_call(
        functools.partial(label_kernel, n),
        out_shape=jax.ShapeDtypeStruct(lab.shape, lab.dtype),
        in_specs=[pl.BlockSpec(memory_space=pltpu.VMEM)],
        out_specs=pl.BlockSpec(memory_space=pltpu.VMEM),
        scratch_shapes=[pltpu.SemaphoreType.DMA((n,)), pltpu.SemaphoreType.DMA((n,))],
        compiler_params=pltpu.CompilerParams(collective_id=2, has_side_effects=True),
    )(lab)


def place_slots(row_ids, owner_map, out_dev):
    table_ids = jnp.arange(owner_map.shape[0], dtype=jnp.int32)
    position = jnp.sum(jnp.where(row_ids[..., None] == table_ids, owner_map, 0), axis=-1)
    target = position // out_dev
    serial = jnp.arange(row_ids.shape[-1], dtype=jnp.int32)
    earlier = (target[..., :, None] == target[..., None, :]) & (serial[:, None] > serial[None, :])
    ranking = jnp.sum(earlier.astype(jnp.int32), axis=-1)
    return (position % out_dev, target, ranking)


def products_kernel(count_ref, order_ref, rows_ref, ks_ref, arrived_ref, panel_ref, init_ref, out_ref):
    out_ref[...] = init_ref[...]
    columns = panel_ref.shape[2]
    side = arrived_ref.shape[2]

    def body(i, carry):
        source = order_ref[i]
        row = rows_ref[source]
        k = ks_ref[source]
        tile = arrived_ref[source]
        for c in range(columns // side):
            cols = pl.ds(c * side, side)
            out_ref[row, :, cols] += jnp.dot(
                tile, panel_ref[k, :, cols], preferred_element_type=jnp.float32
            )
        return carry

    lax.fori_loop(0, count_ref[0], body, 0)


def slot_order(arrived_labels, out_dev):
    rows = arrived_labels[:, 0]
    ks = arrived_labels[:, 1]
    vacant = (rows >= out_dev).astype(jnp.int32)
    order = jnp.argsort(vacant, stable=True).astype(jnp.int32)
    count = jnp.reshape(rows.shape[0] - jnp.sum(vacant), (1,)).astype(jnp.int32)
    return count, order, rows, ks


def add_products(arrived, schedule, panel_tiles, running):
    vmem = pl.BlockSpec(memory_space=pltpu.VMEM)
    smem = pl.BlockSpec(memory_space=pltpu.SMEM)
    return pl.pallas_call(
        products_kernel,
        out_shape=jax.ShapeDtypeStruct(running.shape, jnp.float32),
        in_specs=[smem, smem, smem, smem, vmem, vmem, vmem],
        out_specs=vmem,
        compiler_params=pltpu.CompilerParams(vmem_limit_bytes=48 * 1024 * 1024),
    )(*schedule, arrived, panel_tiles, running)


def per_device(tiles, contraction, row_tile, owner_map, panel):
    wide_count = lax.axis_size("wide")
    tile_dev = tiles.shape[0]
    tile_side = tiles.shape[1]
    out_dev = owner_map.shape[0] // wide_count
    most_slots = tile_dev * 8 // (3 * wide_count)
    slot_total = wide_count * most_slots
    local_row, target, ranking = place_slots(row_tile, owner_map, out_dev)
    slot_index = target * most_slots + ranking
    vacant_label = jnp.stack(
        [jnp.full((slot_total,), out_dev, jnp.int32), jnp.zeros((slot_total,), jnp.int32)], axis=1
    )
    label_out = vacant_label.at[slot_index].set(jnp.stack([local_row, contraction], axis=1))
    packed = jnp.zeros((wide_count, 8, 128), jnp.int32).at[:, 0, :2 * most_slots].set(
        label_out.reshape(wide_count, 2 * most_slots)
    )
    packed = swap_labels(packed, wide_count)
    arrived_labels = packed[:, 0, :2 * most_slots].reshape(wide_count, most_slots, 2)
    grp_count = lax.axis_size("grp")
    pieces = [panel] + [
        lax.ppermute(panel, "grp", [(j, (j + shift) % grp_count) for j in range(grp_count)])
        for shift in range(1, grp_count)
    ]
    gathered = jnp.concatenate(pieces, axis=0)
    panel_tiles = gathered.reshape(gathered.shape[0] // tile_side, tile_side, gathered.shape[1])
    held = panel.shape[0] // tile_side
    owner = arrived_labels[..., 1] // held
    shift = lax.rem(lax.axis_index("grp") - owner + grp_count, grp_count)
    arrived_labels = arrived_labels.at[..., 1].set(shift * held + arrived_labels[..., 1] % held)
    band = tile_side * 5 // 8
    arrived_labels = arrived_labels.reshape(wide_count, most_slots, 2)
    schedules = [slot_order(arrived_labels[:, rank, :], out_dev) for rank in range(most_slots)]
    picks = []
    for rank in range(most_slots):
        chunk_index = jnp.where(ranking == rank, target, wide_count)
        picks.append(jnp.full((wide_count,), tile_dev, jnp.int32).at[chunk_index].set(
            jnp.arange(tile_dev, dtype=jnp.int32), mode="drop"
        ))
    first = jnp.take(tiles, picks[0], axis=0, mode="clip")
    upper_out = jnp.take(tiles[:, :band, :], picks[1], axis=0, mode="clip")
    upper_out, packed = lax.optimization_barrier((upper_out, packed))
    arrived_labels = packed[:, 0, :2 * most_slots].reshape(wide_count, most_slots, 2)
    lower_out = jnp.take(tiles[:, band:, :], picks[1], axis=0, mode="clip")

    def exchange(block):
        return lax.all_to_all(block, "wide", split_axis=0, concat_axis=0, tiled=True)

    zero = jnp.zeros((out_dev, tile_side, gathered.shape[1]), jnp.float32)
    whole = add_products(exchange(first), schedules[0], panel_tiles, zero)
    upper = add_products(exchange(upper_out), schedules[1], panel_tiles, whole[:, :band, :])
    lower_out, whole = lax.optimization_barrier((lower_out, whole))
    arrived = exchange(lower_out)
    upper = ring_sum(upper, lax.axis_size("grp"), 0)
    lower = add_products(arrived, schedules[1], panel_tiles, whole[:, band:, :])
    lower = ring_sum(lower, lax.axis_size("grp"), 1)
    summed = jnp.concatenate([upper, lower], axis=1)
    return summed.reshape(out_dev * tile_side, gathered.shape[1])


def solution(mesh):
    return jax.shard_map(
        per_device,
        mesh=mesh,
        in_specs=(
            P(("grp", "wide"), None, None),
            P(("grp", "wide")),
            P(("grp", "wide")),
            P(),
            P("grp", None),
        ),
        out_specs=P("wide", None),
        check_vma=False,
    )
```

```python
import functools

import jax
import jax.numpy as jnp
from jax import lax
from jax.experimental import pallas as pl
from jax.experimental.pallas import tpu as pltpu
from jax.sharding import PartitionSpec as P


MESH = pl.DeviceIdType.MESH


def ring_sum_kernel(n, x_ref, out_ref, sbuf, rbuf, send_sem, recv_sem):
    me = lax.axis_index("grp")
    column = lax.axis_index("wide")
    right = lax.rem(me + 1, n)
    left = lax.rem(me + n - 1, n)
    half = x_ref.shape[1] // 2
    neighbours = (right, left)

    barrier = pltpu.get_barrier_semaphore()
    for neighbour in (left, right):
        pl.semaphore_signal(barrier, inc=1, device_id=(neighbour, column), device_id_type=MESH)
    pl.semaphore_wait(barrier, 2)

    def send(way, step, src, dst):
        copy = pltpu.make_async_remote_copy(
            src_ref=src,
            dst_ref=dst,
            send_sem=send_sem.at[way, step],
            recv_sem=recv_sem.at[way, step],
            device_id=(neighbours[way], column),
            device_id_type=MESH,
        )
        copy.start()
        return copy

    for step in range(n - 1):
        copies = []
        for way in range(2):
            sign = 1 - 2 * way
            rows = pl.ds(way * half, half)
            chunk = lax.rem(me - sign * (step + 1) + 2 * n, n)
            if step == 0:
                src = x_ref.at[chunk, rows]
            else:
                sbuf[way, step] = rbuf[way, step - 1] + x_ref[chunk, rows]
                src = sbuf.at[way, step]
            copies.append(send(way, step, src, rbuf.at[way, step]))
        for copy in copies:
            copy.wait()

    for way in range(2):
        rows = pl.ds(way * half, half)
        out_ref[me, rows] = rbuf[way, n - 2] + x_ref[me, rows]

    for step in range(n - 1):
        copies = []
        for way in range(2):
            sign = 1 - 2 * way
            rows = pl.ds(way * half, half)
            chunk = lax.rem(me - sign * step + 2 * n, n)
            copies.append(send(way, n - 1 + step, out_ref.at[chunk, rows], out_ref.at[chunk, rows]))
        for copy in copies:
            copy.wait()


def ring_sum(x, n, ident):
    half = x.shape[1] // 2
    return pl.pallas_call(
        functools.partial(ring_sum_kernel, n),
        out_shape=jax.ShapeDtypeStruct(x.shape, x.dtype),
        in_specs=[pl.BlockSpec(memory_space=pltpu.VMEM)],
        out_specs=pl.BlockSpec(memory_space=pltpu.VMEM),
        scratch_shapes=[
            pltpu.VMEM((2, n - 1, half, x.shape[2]), x.dtype),
            pltpu.VMEM((2, n - 1, half, x.shape[2]), x.dtype),
            pltpu.SemaphoreType.DMA((2, 2 * (n - 1))),
            pltpu.SemaphoreType.DMA((2, 2 * (n - 1))),
        ],
        compiler_params=pltpu.CompilerParams(
            collective_id=ident, has_side_effects=True, vmem_limit_bytes=48 * 1024 * 1024
        ),
    )(x)


def label_kernel(n, lab_ref, out_ref, send_sem, recv_sem):
    me = lax.axis_index("wide")
    row = lax.axis_index("grp")
    barrier = pltpu.get_barrier_semaphore()

    def greet(shift, carry):
        peer = lax.rem(me + shift, n)
        pl.semaphore_signal(barrier, inc=1, device_id=(row, peer), device_id_type=MESH)
        return carry

    lax.fori_loop(1, n, greet, 0)
    pl.semaphore_wait(barrier, n - 1)
    out_ref[me] = lab_ref[me]

    def link(source, target, peer):
        return pltpu.make_async_remote_copy(
            src_ref=lab_ref.at[target],
            dst_ref=out_ref.at[source],
            send_sem=send_sem.at[target],
            recv_sem=recv_sem.at[source],
            device_id=(row, peer),
            device_id_type=MESH,
        )

    def start(shift, carry):
        peer = lax.rem(me + shift, n)
        link(me, peer, peer).start()
        return carry

    lax.fori_loop(1, n, start, 0)

    def finish(shift, carry):
        peer = lax.rem(me + shift, n)
        link(me, peer, peer).wait_send()
        source = lax.rem(me + n - shift, n)
        link(source, source, source).wait_recv()
        return carry

    lax.fori_loop(1, n, finish, 0)


def swap_labels(lab, n):
    return pl.pallas_call(
        functools.partial(label_kernel, n),
        out_shape=jax.ShapeDtypeStruct(lab.shape, lab.dtype),
        in_specs=[pl.BlockSpec(memory_space=pltpu.VMEM)],
        out_specs=pl.BlockSpec(memory_space=pltpu.VMEM),
        scratch_shapes=[pltpu.SemaphoreType.DMA((n,)), pltpu.SemaphoreType.DMA((n,))],
        compiler_params=pltpu.CompilerParams(collective_id=2, has_side_effects=True),
    )(lab)


def place_slots(row_ids, owner_map, out_dev):
    table_ids = jnp.arange(owner_map.shape[0], dtype=jnp.int32)
    position = jnp.sum(jnp.where(row_ids[..., None] == table_ids, owner_map, 0), axis=-1)
    target = position // out_dev
    serial = jnp.arange(row_ids.shape[-1], dtype=jnp.int32)
    earlier = (target[..., :, None] == target[..., None, :]) & (serial[:, None] > serial[None, :])
    ranking = jnp.sum(earlier.astype(jnp.int32), axis=-1)
    return (position % out_dev, target, ranking)


def products_kernel(count_ref, order_ref, rows_ref, ks_ref, arrived_ref, panel_ref, init_ref, out_ref):
    out_ref[...] = init_ref[...]
    columns = panel_ref.shape[2]
    side = arrived_ref.shape[2]

    def body(i, carry):
        source = order_ref[i]
        row = rows_ref[source]
        k = ks_ref[source]
        tile = arrived_ref[source]
        for c in range(columns // side):
            cols = pl.ds(c * side, side)
            out_ref[row, :, cols] += jnp.dot(
                tile, panel_ref[k, :, cols], preferred_element_type=jnp.float32
            )
        return carry

    lax.fori_loop(0, count_ref[0], body, 0)


def slot_order(arrived_labels, out_dev):
    rows = arrived_labels[:, 0]
    ks = arrived_labels[:, 1]
    vacant = (rows >= out_dev).astype(jnp.int32)
    order = jnp.argsort(vacant, stable=True).astype(jnp.int32)
    count = jnp.reshape(rows.shape[0] - jnp.sum(vacant), (1,)).astype(jnp.int32)
    return count, order, rows, ks


def add_products(arrived, schedule, panel_tiles, running):
    vmem = pl.BlockSpec(memory_space=pltpu.VMEM)
    smem = pl.BlockSpec(memory_space=pltpu.SMEM)
    return pl.pallas_call(
        products_kernel,
        out_shape=jax.ShapeDtypeStruct(running.shape, jnp.float32),
        in_specs=[smem, smem, smem, smem, vmem, vmem, vmem],
        out_specs=vmem,
        compiler_params=pltpu.CompilerParams(vmem_limit_bytes=48 * 1024 * 1024),
    )(*schedule, arrived, panel_tiles, running)


def per_device(tiles, contraction, row_tile, owner_map, panel):
    wide_count = lax.axis_size("wide")
    tile_dev = tiles.shape[0]
    tile_side = tiles.shape[1]
    out_dev = owner_map.shape[0] // wide_count
    most_slots = tile_dev * 8 // (3 * wide_count)
    slot_total = wide_count * most_slots
    local_row, target, ranking = place_slots(row_tile, owner_map, out_dev)
    slot_index = target * most_slots + ranking
    vacant_label = jnp.stack(
        [jnp.full((slot_total,), out_dev, jnp.int32), jnp.zeros((slot_total,), jnp.int32)], axis=1
    )
    label_out = vacant_label.at[slot_index].set(jnp.stack([local_row, contraction], axis=1))
    packed = jnp.zeros((wide_count, 8, 128), jnp.int32).at[:, 0, :2 * most_slots].set(
        label_out.reshape(wide_count, 2 * most_slots)
    )
    grp_count = lax.axis_size("grp")
    pieces = [panel] + [
        lax.ppermute(panel, "grp", [(j, (j + shift) % grp_count) for j in range(grp_count)])
        for shift in range(1, grp_count)
    ]
    gathered = jnp.concatenate(pieces, axis=0)
    panel_tiles = gathered.reshape(gathered.shape[0] // tile_side, tile_side, gathered.shape[1])
    band = tile_side * 5 // 8
    picks = []
    for rank in range(most_slots):
        chunk_index = jnp.where(ranking == rank, target, wide_count)
        picks.append(jnp.full((wide_count,), tile_dev, jnp.int32).at[chunk_index].set(
            jnp.arange(tile_dev, dtype=jnp.int32), mode="drop"
        ))
    first = jnp.take(tiles, picks[0], axis=0, mode="clip")
    upper_out = jnp.take(tiles[:, :band, :], picks[1], axis=0, mode="clip")
    upper_out, packed = lax.optimization_barrier((upper_out, packed))
    packed = swap_labels(packed, wide_count)
    upper_out, packed = lax.optimization_barrier((upper_out, packed))
    arrived_labels = packed[:, 0, :2 * most_slots].reshape(wide_count, most_slots, 2)
    held = panel.shape[0] // tile_side
    owner = arrived_labels[..., 1] // held
    shift = lax.rem(lax.axis_index("grp") - owner + grp_count, grp_count)
    arrived_labels = arrived_labels.at[..., 1].set(shift * held + arrived_labels[..., 1] % held)
    lower_out = jnp.take(tiles[:, band:, :], picks[1], axis=0, mode="clip")

    schedules = [slot_order(arrived_labels[:, rank, :], out_dev) for rank in range(most_slots)]

    def exchange(block):
        return lax.all_to_all(block, "wide", split_axis=0, concat_axis=0, tiled=True)

    zero = jnp.zeros((out_dev, tile_side, gathered.shape[1]), jnp.float32)
    whole = add_products(exchange(first), schedules[0], panel_tiles, zero)
    upper = add_products(exchange(upper_out), schedules[1], panel_tiles, whole[:, :band, :])
    lower_out, whole = lax.optimization_barrier((lower_out, whole))
    arrived = exchange(lower_out)
    upper = ring_sum(upper, lax.axis_size("grp"), 0)
    lower = add_products(arrived, schedules[1], panel_tiles, whole[:, band:, :])
    lower = ring_sum(lower, lax.axis_size("grp"), 1)
    summed = jnp.concatenate([upper, lower], axis=1)
    return summed.reshape(out_dev * tile_side, gathered.shape[1])


def solution(mesh):
    return jax.shard_map(
        per_device,
        mesh=mesh,
        in_specs=(
            P(("grp", "wide"), None, None),
            P(("grp", "wide")),
            P(("grp", "wide")),
            P(),
            P("grp", None),
        ),
        out_specs=P("wide", None),
        check_vma=False,
    )
```

```python
import functools

import jax
import jax.numpy as jnp
from jax import lax
from jax.experimental import pallas as pl
from jax.experimental.pallas import tpu as pltpu
from jax.sharding import PartitionSpec as P


MESH = pl.DeviceIdType.MESH


def ring_sum_kernel(n, x_ref, out_ref, sbuf, rbuf, send_sem, recv_sem):
    me = lax.axis_index("grp")
    column = lax.axis_index("wide")
    right = lax.rem(me + 1, n)
    left = lax.rem(me + n - 1, n)
    half = x_ref.shape[1] // 2
    neighbours = (right, left)

    barrier = pltpu.get_barrier_semaphore()
    for neighbour in (left, right):
        pl.semaphore_signal(barrier, inc=1, device_id=(neighbour, column), device_id_type=MESH)
    pl.semaphore_wait(barrier, 2)

    def send(way, step, src, dst):
        copy = pltpu.make_async_remote_copy(
            src_ref=src,
            dst_ref=dst,
            send_sem=send_sem.at[way, step],
            recv_sem=recv_sem.at[way, step],
            device_id=(neighbours[way], column),
            device_id_type=MESH,
        )
        copy.start()
        return copy

    sent = []
    for step in range(n - 1):
        copies = []
        for way in range(2):
            sign = 1 - 2 * way
            rows = pl.ds(way * half, half)
            chunk = lax.rem(me - sign * (step + 1) + 2 * n, n)
            if step == 0:
                src = x_ref.at[chunk, rows]
            else:
                sbuf[way, step] = rbuf[way, step - 1] + x_ref[chunk, rows]
                src = sbuf.at[way, step]
            copies.append(send(way, step, src, rbuf.at[way, step]))
        for copy in copies:
            copy.wait_recv()
        sent.extend(copies)

    for way in range(2):
        rows = pl.ds(way * half, half)
        out_ref[me, rows] = rbuf[way, n - 2] + x_ref[me, rows]

    for step in range(n - 1):
        copies = []
        for way in range(2):
            sign = 1 - 2 * way
            rows = pl.ds(way * half, half)
            chunk = lax.rem(me - sign * step + 2 * n, n)
            copies.append(send(way, n - 1 + step, out_ref.at[chunk, rows], out_ref.at[chunk, rows]))
        for copy in copies:
            copy.wait_recv()
        sent.extend(copies)
    for copy in sent:
        copy.wait_send()


def ring_sum(x, n, ident):
    half = x.shape[1] // 2
    return pl.pallas_call(
        functools.partial(ring_sum_kernel, n),
        out_shape=jax.ShapeDtypeStruct(x.shape, x.dtype),
        in_specs=[pl.BlockSpec(memory_space=pltpu.VMEM)],
        out_specs=pl.BlockSpec(memory_space=pltpu.VMEM),
        scratch_shapes=[
            pltpu.VMEM((2, n - 1, half, x.shape[2]), x.dtype),
            pltpu.VMEM((2, n - 1, half, x.shape[2]), x.dtype),
            pltpu.SemaphoreType.DMA((2, 2 * (n - 1))),
            pltpu.SemaphoreType.DMA((2, 2 * (n - 1))),
        ],
        compiler_params=pltpu.CompilerParams(
            collective_id=ident, has_side_effects=True, vmem_limit_bytes=48 * 1024 * 1024
        ),
    )(x)


def label_kernel(n, lab_ref, out_ref, send_sem, recv_sem):
    me = lax.axis_index("wide")
    row = lax.axis_index("grp")
    barrier = pltpu.get_barrier_semaphore()

    def greet(shift, carry):
        peer = lax.rem(me + shift, n)
        pl.semaphore_signal(barrier, inc=1, device_id=(row, peer), device_id_type=MESH)
        return carry

    lax.fori_loop(1, n, greet, 0)
    pl.semaphore_wait(barrier, n - 1)
    out_ref[me] = lab_ref[me]

    def link(source, target, peer):
        return pltpu.make_async_remote_copy(
            src_ref=lab_ref.at[target],
            dst_ref=out_ref.at[source],
            send_sem=send_sem.at[target],
            recv_sem=recv_sem.at[source],
            device_id=(row, peer),
            device_id_type=MESH,
        )

    def start(shift, carry):
        peer = lax.rem(me + shift, n)
        link(me, peer, peer).start()
        return carry

    lax.fori_loop(1, n, start, 0)

    def finish(shift, carry):
        peer = lax.rem(me + shift, n)
        link(me, peer, peer).wait_send()
        source = lax.rem(me + n - shift, n)
        link(source, source, source).wait_recv()
        return carry

    lax.fori_loop(1, n, finish, 0)


def swap_labels(lab, n):
    return pl.pallas_call(
        functools.partial(label_kernel, n),
        out_shape=jax.ShapeDtypeStruct(lab.shape, lab.dtype),
        in_specs=[pl.BlockSpec(memory_space=pltpu.VMEM)],
        out_specs=pl.BlockSpec(memory_space=pltpu.VMEM),
        scratch_shapes=[pltpu.SemaphoreType.DMA((n,)), pltpu.SemaphoreType.DMA((n,))],
        compiler_params=pltpu.CompilerParams(collective_id=2, has_side_effects=True),
    )(lab)


def place_slots(row_ids, owner_map, out_dev):
    table_ids = jnp.arange(owner_map.shape[0], dtype=jnp.int32)
    position = jnp.sum(jnp.where(row_ids[..., None] == table_ids, owner_map, 0), axis=-1)
    target = position // out_dev
    serial = jnp.arange(row_ids.shape[-1], dtype=jnp.int32)
    earlier = (target[..., :, None] == target[..., None, :]) & (serial[:, None] > serial[None, :])
    ranking = jnp.sum(earlier.astype(jnp.int32), axis=-1)
    return (position % out_dev, target, ranking)


def products_kernel(count_ref, order_ref, rows_ref, ks_ref, arrived_ref, panel_ref, init_ref, out_ref):
    out_ref[...] = init_ref[...]
    columns = panel_ref.shape[2]
    side = arrived_ref.shape[2]

    def body(i, carry):
        source = order_ref[i]
        row = rows_ref[source]
        k = ks_ref[source]
        tile = arrived_ref[source]
        for c in range(columns // side):
            cols = pl.ds(c * side, side)
            out_ref[row, :, cols] += jnp.dot(
                tile, panel_ref[k, :, cols], preferred_element_type=jnp.float32
            )
        return carry

    lax.fori_loop(0, count_ref[0], body, 0)


def slot_order(arrived_labels, out_dev):
    rows = arrived_labels[:, 0]
    ks = arrived_labels[:, 1]
    vacant = (rows >= out_dev).astype(jnp.int32)
    order = jnp.argsort(vacant, stable=True).astype(jnp.int32)
    count = jnp.reshape(rows.shape[0] - jnp.sum(vacant), (1,)).astype(jnp.int32)
    return count, order, rows, ks


def add_products(arrived, schedule, panel_tiles, running):
    vmem = pl.BlockSpec(memory_space=pltpu.VMEM)
    smem = pl.BlockSpec(memory_space=pltpu.SMEM)
    return pl.pallas_call(
        products_kernel,
        out_shape=jax.ShapeDtypeStruct(running.shape, jnp.float32),
        in_specs=[smem, smem, smem, smem, vmem, vmem, vmem],
        out_specs=vmem,
        compiler_params=pltpu.CompilerParams(vmem_limit_bytes=48 * 1024 * 1024),
    )(*schedule, arrived, panel_tiles, running)


def per_device(tiles, contraction, row_tile, owner_map, panel):
    wide_count = lax.axis_size("wide")
    tile_dev = tiles.shape[0]
    tile_side = tiles.shape[1]
    out_dev = owner_map.shape[0] // wide_count
    most_slots = tile_dev * 8 // (3 * wide_count)
    slot_total = wide_count * most_slots
    local_row, target, ranking = place_slots(row_tile, owner_map, out_dev)
    slot_index = target * most_slots + ranking
    vacant_label = jnp.stack(
        [jnp.full((slot_total,), out_dev, jnp.int32), jnp.zeros((slot_total,), jnp.int32)], axis=1
    )
    label_out = vacant_label.at[slot_index].set(jnp.stack([local_row, contraction], axis=1))
    packed = jnp.zeros((wide_count, 8, 128), jnp.int32).at[:, 0, :2 * most_slots].set(
        label_out.reshape(wide_count, 2 * most_slots)
    )
    grp_count = lax.axis_size("grp")
    pieces = [panel] + [
        lax.ppermute(panel, "grp", [(j, (j + shift) % grp_count) for j in range(grp_count)])
        for shift in range(1, grp_count)
    ]
    gathered = jnp.concatenate(pieces, axis=0)
    panel_tiles = gathered.reshape(gathered.shape[0] // tile_side, tile_side, gathered.shape[1])
    band = tile_side * 11 // 16
    picks = []
    for rank in range(most_slots):
        chunk_index = jnp.where(ranking == rank, target, wide_count)
        picks.append(jnp.full((wide_count,), tile_dev, jnp.int32).at[chunk_index].set(
            jnp.arange(tile_dev, dtype=jnp.int32), mode="drop"
        ))
    first = jnp.take(tiles, picks[0], axis=0, mode="clip")
    upper_out = jnp.take(tiles[:, :band, :], picks[1], axis=0, mode="clip")
    upper_out, packed = lax.optimization_barrier((upper_out, packed))
    packed = swap_labels(packed, wide_count)
    upper_out, packed = lax.optimization_barrier((upper_out, packed))
    arrived_labels = packed[:, 0, :2 * most_slots].reshape(wide_count, most_slots, 2)
    held = panel.shape[0] // tile_side
    owner = arrived_labels[..., 1] // held
    shift = lax.rem(lax.axis_index("grp") - owner + grp_count, grp_count)
    arrived_labels = arrived_labels.at[..., 1].set(shift * held + arrived_labels[..., 1] % held)
    lower_out = jnp.take(tiles[:, band:, :], picks[1], axis=0, mode="clip")

    schedules = [slot_order(arrived_labels[:, rank, :], out_dev) for rank in range(most_slots)]

    def exchange(block):
        return lax.all_to_all(block, "wide", split_axis=0, concat_axis=0, tiled=True)

    zero = jnp.zeros((out_dev, tile_side, gathered.shape[1]), jnp.float32)
    whole = add_products(exchange(first), schedules[0], panel_tiles, zero)
    upper = add_products(exchange(upper_out), schedules[1], panel_tiles, whole[:, :band, :])
    lower_out, whole = lax.optimization_barrier((lower_out, whole))
    arrived = exchange(lower_out)
    upper = ring_sum(upper, lax.axis_size("grp"), 0)
    lower = add_products(arrived, schedules[1], panel_tiles, whole[:, band:, :])
    lower = ring_sum(lower, lax.axis_size("grp"), 1)
    summed = jnp.concatenate([upper, lower], axis=1)
    return summed.reshape(out_dev * tile_side, gathered.shape[1])


def solution(mesh):
    return jax.shard_map(
        per_device,
        mesh=mesh,
        in_specs=(
            P(("grp", "wide"), None, None),
            P(("grp", "wide")),
            P(("grp", "wide")),
            P(),
            P("grp", None),
        ),
        out_specs=P("wide", None),
        check_vma=False,
    )
```

```python
import functools

import jax
import jax.numpy as jnp
from jax import lax
from jax.experimental import pallas as pl
from jax.experimental.pallas import tpu as pltpu
from jax.sharding import PartitionSpec as P


MESH = pl.DeviceIdType.MESH


def ring_sum_kernel(n, x_ref, out_ref, sbuf, rbuf, send_sem, recv_sem):
    me = lax.axis_index("grp")
    column = lax.axis_index("wide")
    right = lax.rem(me + 1, n)
    left = lax.rem(me + n - 1, n)
    half = x_ref.shape[1] // 2
    neighbours = (right, left)

    barrier = pltpu.get_barrier_semaphore()
    for neighbour in (left, right):
        pl.semaphore_signal(barrier, inc=1, device_id=(neighbour, column), device_id_type=MESH)
    pl.semaphore_wait(barrier, 2)

    def send(way, step, src, dst):
        copy = pltpu.make_async_remote_copy(
            src_ref=src,
            dst_ref=dst,
            send_sem=send_sem.at[way, step],
            recv_sem=recv_sem.at[way, step],
            device_id=(neighbours[way], column),
            device_id_type=MESH,
        )
        copy.start()
        return copy

    sent = []
    for step in range(n - 1):
        copies = []
        for way in range(2):
            sign = 1 - 2 * way
            rows = pl.ds(way * half, half)
            chunk = lax.rem(me - sign * (step + 1) + 2 * n, n)
            if step == 0:
                src = x_ref.at[chunk, rows]
            else:
                sbuf[way, step] = rbuf[way, step - 1] + x_ref[chunk, rows]
                src = sbuf.at[way, step]
            copies.append(send(way, step, src, rbuf.at[way, step]))
        for copy in copies:
            copy.wait_recv()
        sent.extend(copies)

    for way in range(2):
        rows = pl.ds(way * half, half)
        out_ref[me, rows] = rbuf[way, n - 2] + x_ref[me, rows]

    for step in range(n - 1):
        copies = []
        for way in range(2):
            sign = 1 - 2 * way
            rows = pl.ds(way * half, half)
            chunk = lax.rem(me - sign * step + 2 * n, n)
            copies.append(send(way, n - 1 + step, out_ref.at[chunk, rows], out_ref.at[chunk, rows]))
        for copy in copies:
            copy.wait_recv()
        sent.extend(copies)
    for copy in sent:
        copy.wait_send()


def ring_sum(x, n, ident):
    half = x.shape[1] // 2
    return pl.pallas_call(
        functools.partial(ring_sum_kernel, n),
        out_shape=jax.ShapeDtypeStruct(x.shape, x.dtype),
        in_specs=[pl.BlockSpec(memory_space=pltpu.VMEM)],
        out_specs=pl.BlockSpec(memory_space=pltpu.VMEM),
        scratch_shapes=[
            pltpu.VMEM((2, n - 1, half, x.shape[2]), x.dtype),
            pltpu.VMEM((2, n - 1, half, x.shape[2]), x.dtype),
            pltpu.SemaphoreType.DMA((2, 2 * (n - 1))),
            pltpu.SemaphoreType.DMA((2, 2 * (n - 1))),
        ],
        compiler_params=pltpu.CompilerParams(
            collective_id=ident, has_side_effects=True, vmem_limit_bytes=48 * 1024 * 1024
        ),
    )(x)


def label_kernel(n, lab_ref, out_ref, send_sem, recv_sem):
    me = lax.axis_index("wide")
    row = lax.axis_index("grp")
    barrier = pltpu.get_barrier_semaphore()

    def greet(shift, carry):
        peer = lax.rem(me + shift, n)
        pl.semaphore_signal(barrier, inc=1, device_id=(row, peer), device_id_type=MESH)
        return carry

    lax.fori_loop(1, n, greet, 0)
    pl.semaphore_wait(barrier, n - 1)
    out_ref[me] = lab_ref[me]

    def link(source, target, peer):
        return pltpu.make_async_remote_copy(
            src_ref=lab_ref.at[target],
            dst_ref=out_ref.at[source],
            send_sem=send_sem.at[target],
            recv_sem=recv_sem.at[source],
            device_id=(row, peer),
            device_id_type=MESH,
        )

    def start(shift, carry):
        peer = lax.rem(me + shift, n)
        link(me, peer, peer).start()
        return carry

    lax.fori_loop(1, n, start, 0)

    def finish(shift, carry):
        peer = lax.rem(me + shift, n)
        link(me, peer, peer).wait_send()
        source = lax.rem(me + n - shift, n)
        link(source, source, source).wait_recv()
        return carry

    lax.fori_loop(1, n, finish, 0)


def swap_labels(lab, n):
    return pl.pallas_call(
        functools.partial(label_kernel, n),
        out_shape=jax.ShapeDtypeStruct(lab.shape, lab.dtype),
        in_specs=[pl.BlockSpec(memory_space=pltpu.VMEM)],
        out_specs=pl.BlockSpec(memory_space=pltpu.VMEM),
        scratch_shapes=[pltpu.SemaphoreType.DMA((n,)), pltpu.SemaphoreType.DMA((n,))],
        compiler_params=pltpu.CompilerParams(collective_id=2, has_side_effects=True),
    )(lab)


def place_slots(row_ids, owner_map, out_dev):
    table_ids = jnp.arange(owner_map.shape[0], dtype=jnp.int32)
    position = jnp.sum(jnp.where(row_ids[..., None] == table_ids, owner_map, 0), axis=-1)
    target = position // out_dev
    serial = jnp.arange(row_ids.shape[-1], dtype=jnp.int32)
    earlier = (target[..., :, None] == target[..., None, :]) & (serial[:, None] > serial[None, :])
    ranking = jnp.sum(earlier.astype(jnp.int32), axis=-1)
    return (position % out_dev, target, ranking)


def products_kernel(count_ref, order_ref, rows_ref, ks_ref, arrived_ref, panel_ref, init_ref, out_ref):
    out_ref[...] = init_ref[...]
    columns = panel_ref.shape[2]
    side = arrived_ref.shape[2]

    def body(i, carry):
        source = order_ref[i]
        row = rows_ref[source]
        k = ks_ref[source]
        tile = arrived_ref[source]
        for c in range(columns // side):
            cols = pl.ds(c * side, side)
            out_ref[row, :, cols] += jnp.dot(
                tile, panel_ref[k, :, cols], preferred_element_type=jnp.float32
            )
        return carry

    lax.fori_loop(0, count_ref[0], body, 0)


def slot_order(arrived_labels, out_dev):
    rows = arrived_labels[:, 0]
    ks = arrived_labels[:, 1]
    vacant = (rows >= out_dev).astype(jnp.int32)
    order = jnp.argsort(vacant, stable=True).astype(jnp.int32)
    count = jnp.reshape(rows.shape[0] - jnp.sum(vacant), (1,)).astype(jnp.int32)
    return count, order, rows, ks


def add_products(arrived, schedule, panel_tiles, running):
    vmem = pl.BlockSpec(memory_space=pltpu.VMEM)
    smem = pl.BlockSpec(memory_space=pltpu.SMEM)
    return pl.pallas_call(
        products_kernel,
        out_shape=jax.ShapeDtypeStruct(running.shape, jnp.float32),
        in_specs=[smem, smem, smem, smem, vmem, vmem, vmem],
        out_specs=vmem,
        compiler_params=pltpu.CompilerParams(vmem_limit_bytes=48 * 1024 * 1024),
    )(*schedule, arrived, panel_tiles, running)


def per_device(tiles, contraction, row_tile, owner_map, panel):
    wide_count = lax.axis_size("wide")
    tile_dev = tiles.shape[0]
    tile_side = tiles.shape[1]
    out_dev = owner_map.shape[0] // wide_count
    most_slots = tile_dev * 8 // (3 * wide_count)
    slot_total = wide_count * most_slots
    local_row, target, ranking = place_slots(row_tile, owner_map, out_dev)
    slot_index = target * most_slots + ranking
    vacant_label = jnp.stack(
        [jnp.full((slot_total,), out_dev, jnp.int32), jnp.zeros((slot_total,), jnp.int32)], axis=1
    )
    label_out = vacant_label.at[slot_index].set(jnp.stack([local_row, contraction], axis=1))
    packed = jnp.zeros((wide_count, 8, 128), jnp.int32).at[:, 0, :2 * most_slots].set(
        label_out.reshape(wide_count, 2 * most_slots)
    )
    grp_count = lax.axis_size("grp")
    pieces = [panel] + [
        lax.ppermute(panel, "grp", [(j, (j + shift) % grp_count) for j in range(grp_count)])
        for shift in range(1, grp_count)
    ]
    gathered = jnp.concatenate(pieces, axis=0)
    panel_tiles = gathered.reshape(gathered.shape[0] // tile_side, tile_side, gathered.shape[1])
    band = tile_side * 5 // 8
    picks = []
    for rank in range(most_slots):
        chunk_index = jnp.where(ranking == rank, target, wide_count)
        picks.append(jnp.full((wide_count,), tile_dev, jnp.int32).at[chunk_index].set(
            jnp.arange(tile_dev, dtype=jnp.int32), mode="drop"
        ))
    first = jnp.take(tiles, picks[0], axis=0, mode="clip")
    upper_out = jnp.take(tiles[:, :band, :], picks[1], axis=0, mode="clip")
    upper_out, packed = lax.optimization_barrier((upper_out, packed))
    packed = swap_labels(packed, wide_count)
    upper_out, packed = lax.optimization_barrier((upper_out, packed))
    arrived_labels = packed[:, 0, :2 * most_slots].reshape(wide_count, most_slots, 2)
    held = panel.shape[0] // tile_side
    owner = arrived_labels[..., 1] // held
    shift = lax.rem(lax.axis_index("grp") - owner + grp_count, grp_count)
    arrived_labels = arrived_labels.at[..., 1].set(shift * held + arrived_labels[..., 1] % held)
    lower_out = jnp.take(tiles[:, band:, :], picks[1], axis=0, mode="clip")

    schedules = [slot_order(arrived_labels[:, rank, :], out_dev) for rank in range(most_slots)]

    def exchange(block):
        return lax.all_to_all(block, "wide", split_axis=0, concat_axis=0, tiled=True)

    zero = jnp.zeros((out_dev, tile_side, gathered.shape[1]), jnp.float32)
    whole = add_products(exchange(first), schedules[0], panel_tiles, zero)
    upper = add_products(exchange(upper_out), schedules[1], panel_tiles, whole[:, :band, :])
    lower_out, whole = lax.optimization_barrier((lower_out, whole))
    arrived = exchange(lower_out)
    upper = ring_sum(upper, lax.axis_size("grp"), 0)
    lower = add_products(arrived, schedules[1], panel_tiles, whole[:, band:, :])
    lower = ring_sum(lower, lax.axis_size("grp"), 1)
    summed = jnp.concatenate([upper, lower], axis=1)
    return summed.reshape(out_dev * tile_side, gathered.shape[1])


def solution(mesh):
    return jax.shard_map(
        per_device,
        mesh=mesh,
        in_specs=(
            P(("grp", "wide"), None, None),
            P(("grp", "wide")),
            P(("grp", "wide")),
            P(),
            P("grp", None),
        ),
        out_specs=P("wide", None),
        check_vma=False,
    )
```

```python
import functools

import jax
import jax.numpy as jnp
from jax import lax
from jax.experimental import pallas as pl
from jax.experimental.pallas import tpu as pltpu
from jax.sharding import PartitionSpec as P


MESH = pl.DeviceIdType.MESH


def ring_sum_kernel(n, x_ref, out_ref, sbuf, rbuf, send_sem, recv_sem):
    me = lax.axis_index("grp")
    column = lax.axis_index("wide")
    right = lax.rem(me + 1, n)
    left = lax.rem(me + n - 1, n)
    half = x_ref.shape[1] // 2
    neighbours = (right, left)

    barrier = pltpu.get_barrier_semaphore()
    for neighbour in (left, right):
        pl.semaphore_signal(barrier, inc=1, device_id=(neighbour, column), device_id_type=MESH)
    pl.semaphore_wait(barrier, 2)

    def send(way, step, src, dst):
        copy = pltpu.make_async_remote_copy(
            src_ref=src,
            dst_ref=dst,
            send_sem=send_sem.at[way, step],
            recv_sem=recv_sem.at[way, step],
            device_id=(neighbours[way], column),
            device_id_type=MESH,
        )
        copy.start()
        return copy

    for step in range(n - 1):
        copies = []
        for way in range(2):
            sign = 1 - 2 * way
            rows = pl.ds(way * half, half)
            chunk = lax.rem(me - sign * (step + 1) + 2 * n, n)
            if step == 0:
                src = x_ref.at[chunk, rows]
            else:
                sbuf[way, step] = rbuf[way, step - 1] + x_ref[chunk, rows]
                src = sbuf.at[way, step]
            copies.append(send(way, step, src, rbuf.at[way, step]))
        for copy in copies:
            copy.wait()

    for way in range(2):
        rows = pl.ds(way * half, half)
        out_ref[me, rows] = rbuf[way, n - 2] + x_ref[me, rows]

    for step in range(n - 1):
        copies = []
        for way in range(2):
            sign = 1 - 2 * way
            rows = pl.ds(way * half, half)
            chunk = lax.rem(me - sign * step + 2 * n, n)
            copies.append(send(way, n - 1 + step, out_ref.at[chunk, rows], out_ref.at[chunk, rows]))
        for copy in copies:
            copy.wait()


def ring_sum(x, n, ident):
    half = x.shape[1] // 2
    return pl.pallas_call(
        functools.partial(ring_sum_kernel, n),
        out_shape=jax.ShapeDtypeStruct(x.shape, x.dtype),
        in_specs=[pl.BlockSpec(memory_space=pltpu.VMEM)],
        out_specs=pl.BlockSpec(memory_space=pltpu.VMEM),
        scratch_shapes=[
            pltpu.VMEM((2, n - 1, half, x.shape[2]), x.dtype),
            pltpu.VMEM((2, n - 1, half, x.shape[2]), x.dtype),
            pltpu.SemaphoreType.DMA((2, 2 * (n - 1))),
            pltpu.SemaphoreType.DMA((2, 2 * (n - 1))),
        ],
        compiler_params=pltpu.CompilerParams(
            collective_id=ident, has_side_effects=True, vmem_limit_bytes=48 * 1024 * 1024
        ),
    )(x)


def label_kernel(n, lab_ref, out_ref, send_sem, recv_sem):
    me = lax.axis_index("wide")
    row = lax.axis_index("grp")
    barrier = pltpu.get_barrier_semaphore()

    def greet(shift, carry):
        peer = lax.rem(me + shift, n)
        pl.semaphore_signal(barrier, inc=1, device_id=(row, peer), device_id_type=MESH)
        return carry

    lax.fori_loop(1, n, greet, 0)
    pl.semaphore_wait(barrier, n - 1)
    out_ref[me] = lab_ref[me]

    def link(source, target, peer):
        return pltpu.make_async_remote_copy(
            src_ref=lab_ref.at[target],
            dst_ref=out_ref.at[source],
            send_sem=send_sem.at[target],
            recv_sem=recv_sem.at[source],
            device_id=(row, peer),
            device_id_type=MESH,
        )

    def start(shift, carry):
        peer = lax.rem(me + shift, n)
        link(me, peer, peer).start()
        return carry

    lax.fori_loop(1, n, start, 0)

    def finish(shift, carry):
        peer = lax.rem(me + shift, n)
        link(me, peer, peer).wait_send()
        source = lax.rem(me + n - shift, n)
        link(source, source, source).wait_recv()
        return carry

    lax.fori_loop(1, n, finish, 0)


def swap_labels(lab, n):
    return pl.pallas_call(
        functools.partial(label_kernel, n),
        out_shape=jax.ShapeDtypeStruct(lab.shape, lab.dtype),
        in_specs=[pl.BlockSpec(memory_space=pltpu.VMEM)],
        out_specs=pl.BlockSpec(memory_space=pltpu.VMEM),
        scratch_shapes=[pltpu.SemaphoreType.DMA((n,)), pltpu.SemaphoreType.DMA((n,))],
        compiler_params=pltpu.CompilerParams(collective_id=2, has_side_effects=True),
    )(lab)


def place_slots(row_ids, owner_map, out_dev):
    table_ids = jnp.arange(owner_map.shape[0], dtype=jnp.int32)
    position = jnp.sum(jnp.where(row_ids[..., None] == table_ids, owner_map, 0), axis=-1)
    target = position // out_dev
    serial = jnp.arange(row_ids.shape[-1], dtype=jnp.int32)
    earlier = (target[..., :, None] == target[..., None, :]) & (serial[:, None] > serial[None, :])
    ranking = jnp.sum(earlier.astype(jnp.int32), axis=-1)
    return (position % out_dev, target, ranking)


def products_kernel(count_ref, order_ref, rows_ref, ks_ref, arrived_ref, panel_ref, init_ref, out_ref):
    out_ref[...] = init_ref[...]
    columns = panel_ref.shape[2]
    side = arrived_ref.shape[2]

    def body(i, carry):
        source = order_ref[i]
        row = rows_ref[source]
        k = ks_ref[source]
        tile = arrived_ref[source]
        for c in range(columns // side):
            cols = pl.ds(c * side, side)
            out_ref[row, :, cols] += jnp.dot(
                tile, panel_ref[k, :, cols], preferred_element_type=jnp.float32
            )
        return carry

    lax.fori_loop(0, count_ref[0], body, 0)


def slot_order(arrived_labels, out_dev):
    rows = arrived_labels[:, 0]
    ks = arrived_labels[:, 1]
    vacant = (rows >= out_dev).astype(jnp.int32)
    order = jnp.argsort(vacant, stable=True).astype(jnp.int32)
    count = jnp.reshape(rows.shape[0] - jnp.sum(vacant), (1,)).astype(jnp.int32)
    return count, order, rows, ks


def add_products(arrived, schedule, panel_tiles, running):
    vmem = pl.BlockSpec(memory_space=pltpu.VMEM)
    smem = pl.BlockSpec(memory_space=pltpu.SMEM)
    return pl.pallas_call(
        products_kernel,
        out_shape=jax.ShapeDtypeStruct(running.shape, jnp.float32),
        in_specs=[smem, smem, smem, smem, vmem, vmem, vmem],
        out_specs=vmem,
        compiler_params=pltpu.CompilerParams(vmem_limit_bytes=48 * 1024 * 1024),
    )(*schedule, arrived, panel_tiles, running)


def per_device(tiles, contraction, row_tile, owner_map, panel):
    wide_count = lax.axis_size("wide")
    tile_dev = tiles.shape[0]
    tile_side = tiles.shape[1]
    out_dev = owner_map.shape[0] // wide_count
    most_slots = tile_dev * 8 // (3 * wide_count)
    slot_total = wide_count * most_slots
    local_row, target, ranking = place_slots(row_tile, owner_map, out_dev)
    slot_index = target * most_slots + ranking
    vacant_label = jnp.stack(
        [jnp.full((slot_total,), out_dev, jnp.int32), jnp.zeros((slot_total,), jnp.int32)], axis=1
    )
    label_out = vacant_label.at[slot_index].set(jnp.stack([local_row, contraction], axis=1))
    packed = jnp.zeros((wide_count, 8, 128), jnp.int32).at[:, 0, :2 * most_slots].set(
        label_out.reshape(wide_count, 2 * most_slots)
    )
    grp_count = lax.axis_size("grp")
    pieces = [panel] + [
        lax.ppermute(panel, "grp", [(j, (j + shift) % grp_count) for j in range(grp_count)])
        for shift in range(1, grp_count)
    ]
    gathered = jnp.concatenate(pieces, axis=0)
    panel_tiles = gathered.reshape(gathered.shape[0] // tile_side, tile_side, gathered.shape[1])
    band = tile_side * 5 // 8
    picks = []
    for rank in range(most_slots):
        chunk_index = jnp.where(ranking == rank, target, wide_count)
        picks.append(jnp.full((wide_count,), tile_dev, jnp.int32).at[chunk_index].set(
            jnp.arange(tile_dev, dtype=jnp.int32), mode="drop"
        ))
    first = jnp.take(tiles, picks[0], axis=0, mode="clip")
    upper_out = jnp.take(tiles[:, :band, :], picks[1], axis=0, mode="clip")
    packed = swap_labels(packed, wide_count)
    first, packed = lax.optimization_barrier((first, packed))
    arrived_labels = packed[:, 0, :2 * most_slots].reshape(wide_count, most_slots, 2)
    held = panel.shape[0] // tile_side
    owner = arrived_labels[..., 1] // held
    shift = lax.rem(lax.axis_index("grp") - owner + grp_count, grp_count)
    arrived_labels = arrived_labels.at[..., 1].set(shift * held + arrived_labels[..., 1] % held)
    lower_out = jnp.take(tiles[:, band:, :], picks[1], axis=0, mode="clip")

    schedules = [slot_order(arrived_labels[:, rank, :], out_dev) for rank in range(most_slots)]

    def exchange(block):
        return lax.all_to_all(block, "wide", split_axis=0, concat_axis=0, tiled=True)

    zero = jnp.zeros((out_dev, tile_side, gathered.shape[1]), jnp.float32)
    whole = add_products(exchange(first), schedules[0], panel_tiles, zero)
    upper = add_products(exchange(upper_out), schedules[1], panel_tiles, whole[:, :band, :])
    lower_out, whole = lax.optimization_barrier((lower_out, whole))
    arrived = exchange(lower_out)
    upper = ring_sum(upper, lax.axis_size("grp"), 0)
    lower = add_products(arrived, schedules[1], panel_tiles, whole[:, band:, :])
    lower = ring_sum(lower, lax.axis_size("grp"), 1)
    summed = jnp.concatenate([upper, lower], axis=1)
    return summed.reshape(out_dev * tile_side, gathered.shape[1])


def solution(mesh):
    return jax.shard_map(
        per_device,
        mesh=mesh,
        in_specs=(
            P(("grp", "wide"), None, None),
            P(("grp", "wide")),
            P(("grp", "wide")),
            P(),
            P("grp", None),
        ),
        out_specs=P("wide", None),
        check_vma=False,
    )
```

```python
import functools

import jax
import jax.numpy as jnp
from jax import lax
from jax.experimental import pallas as pl
from jax.experimental.pallas import tpu as pltpu
from jax.sharding import PartitionSpec as P


MESH = pl.DeviceIdType.MESH


def ring_sum_kernel(n, x_ref, out_ref, sbuf, rbuf, send_sem, recv_sem):
    me = lax.axis_index("grp")
    column = lax.axis_index("wide")
    right = lax.rem(me + 1, n)
    left = lax.rem(me + n - 1, n)
    half = x_ref.shape[1] // 2
    neighbours = (right, left)

    barrier = pltpu.get_barrier_semaphore()
    for neighbour in (left, right):
        pl.semaphore_signal(barrier, inc=1, device_id=(neighbour, column), device_id_type=MESH)
    pl.semaphore_wait(barrier, 2)

    def send(way, step, src, dst):
        copy = pltpu.make_async_remote_copy(
            src_ref=src,
            dst_ref=dst,
            send_sem=send_sem.at[way, step],
            recv_sem=recv_sem.at[way, step],
            device_id=(neighbours[way], column),
            device_id_type=MESH,
        )
        copy.start()
        return copy

    for step in range(n - 1):
        copies = []
        for way in range(2):
            sign = 1 - 2 * way
            rows = pl.ds(way * half, half)
            chunk = lax.rem(me - sign * (step + 1) + 2 * n, n)
            if step == 0:
                src = x_ref.at[chunk, rows]
            else:
                sbuf[way, step] = rbuf[way, step - 1] + x_ref[chunk, rows]
                src = sbuf.at[way, step]
            copies.append(send(way, step, src, rbuf.at[way, step]))
        for copy in copies:
            copy.wait()

    for way in range(2):
        rows = pl.ds(way * half, half)
        out_ref[me, rows] = rbuf[way, n - 2] + x_ref[me, rows]

    for step in range(n - 1):
        copies = []
        for way in range(2):
            sign = 1 - 2 * way
            rows = pl.ds(way * half, half)
            chunk = lax.rem(me - sign * step + 2 * n, n)
            copies.append(send(way, n - 1 + step, out_ref.at[chunk, rows], out_ref.at[chunk, rows]))
        for copy in copies:
            copy.wait()


def ring_sum(x, n, ident):
    half = x.shape[1] // 2
    return pl.pallas_call(
        functools.partial(ring_sum_kernel, n),
        out_shape=jax.ShapeDtypeStruct(x.shape, x.dtype),
        in_specs=[pl.BlockSpec(memory_space=pltpu.VMEM)],
        out_specs=pl.BlockSpec(memory_space=pltpu.VMEM),
        scratch_shapes=[
            pltpu.VMEM((2, n - 1, half, x.shape[2]), x.dtype),
            pltpu.VMEM((2, n - 1, half, x.shape[2]), x.dtype),
            pltpu.SemaphoreType.DMA((2, 2 * (n - 1))),
            pltpu.SemaphoreType.DMA((2, 2 * (n - 1))),
        ],
        compiler_params=pltpu.CompilerParams(
            collective_id=ident, has_side_effects=True, vmem_limit_bytes=48 * 1024 * 1024
        ),
    )(x)


def label_kernel(n, lab_ref, out_ref, send_sem, recv_sem):
    me = lax.axis_index("wide")
    row = lax.axis_index("grp")
    barrier = pltpu.get_barrier_semaphore()

    def greet(shift, carry):
        peer = lax.rem(me + shift, n)
        pl.semaphore_signal(barrier, inc=1, device_id=(row, peer), device_id_type=MESH)
        return carry

    lax.fori_loop(1, n, greet, 0)
    pl.semaphore_wait(barrier, n - 1)
    out_ref[me] = lab_ref[me]

    def link(source, target, peer):
        return pltpu.make_async_remote_copy(
            src_ref=lab_ref.at[target],
            dst_ref=out_ref.at[source],
            send_sem=send_sem.at[target],
            recv_sem=recv_sem.at[source],
            device_id=(row, peer),
            device_id_type=MESH,
        )

    def start(shift, carry):
        peer = lax.rem(me + shift, n)
        link(me, peer, peer).start()
        return carry

    lax.fori_loop(1, n, start, 0)

    def finish(shift, carry):
        peer = lax.rem(me + shift, n)
        link(me, peer, peer).wait_send()
        source = lax.rem(me + n - shift, n)
        link(source, source, source).wait_recv()
        return carry

    lax.fori_loop(1, n, finish, 0)


def swap_labels(lab, n):
    return pl.pallas_call(
        functools.partial(label_kernel, n),
        out_shape=jax.ShapeDtypeStruct(lab.shape, lab.dtype),
        in_specs=[pl.BlockSpec(memory_space=pltpu.VMEM)],
        out_specs=pl.BlockSpec(memory_space=pltpu.VMEM),
        scratch_shapes=[pltpu.SemaphoreType.DMA((n,)), pltpu.SemaphoreType.DMA((n,))],
        compiler_params=pltpu.CompilerParams(collective_id=2, has_side_effects=True),
    )(lab)


def place_slots(row_ids, owner_map, out_dev):
    table_ids = jnp.arange(owner_map.shape[0], dtype=jnp.int32)
    position = jnp.sum(jnp.where(row_ids[..., None] == table_ids, owner_map, 0), axis=-1)
    target = position // out_dev
    serial = jnp.arange(row_ids.shape[-1], dtype=jnp.int32)
    earlier = (target[..., :, None] == target[..., None, :]) & (serial[:, None] > serial[None, :])
    ranking = jnp.sum(earlier.astype(jnp.int32), axis=-1)
    return (position % out_dev, target, ranking)


def products_kernel(count_ref, order_ref, rows_ref, ks_ref, arrived_ref, panel_ref, init_ref, out_ref):
    del init_ref
    columns = panel_ref.shape[2]
    side = arrived_ref.shape[2]

    def body(i, carry):
        source = order_ref[i]
        row = rows_ref[source]
        k = ks_ref[source]
        tile = arrived_ref[source]
        for c in range(columns // side):
            cols = pl.ds(c * side, side)
            out_ref[row, :, cols] += jnp.dot(
                tile, panel_ref[k, :, cols], preferred_element_type=jnp.float32
            )
        return carry

    lax.fori_loop(0, count_ref[0], body, 0)


def slot_order(arrived_labels, out_dev):
    rows = arrived_labels[:, 0]
    ks = arrived_labels[:, 1]
    vacant = (rows >= out_dev).astype(jnp.int32)
    order = jnp.argsort(vacant, stable=True).astype(jnp.int32)
    count = jnp.reshape(rows.shape[0] - jnp.sum(vacant), (1,)).astype(jnp.int32)
    return count, order, rows, ks


def add_products(arrived, schedule, panel_tiles, running):
    vmem = pl.BlockSpec(memory_space=pltpu.VMEM)
    smem = pl.BlockSpec(memory_space=pltpu.SMEM)
    return pl.pallas_call(
        products_kernel,
        out_shape=jax.ShapeDtypeStruct(running.shape, jnp.float32),
        in_specs=[smem, smem, smem, smem, vmem, vmem, vmem],
        out_specs=vmem,
        input_output_aliases={6: 0},
        compiler_params=pltpu.CompilerParams(vmem_limit_bytes=48 * 1024 * 1024),
    )(*schedule, arrived, panel_tiles, running)


def per_device(tiles, contraction, row_tile, owner_map, panel):
    wide_count = lax.axis_size("wide")
    tile_dev = tiles.shape[0]
    tile_side = tiles.shape[1]
    out_dev = owner_map.shape[0] // wide_count
    most_slots = tile_dev * 8 // (3 * wide_count)
    slot_total = wide_count * most_slots
    local_row, target, ranking = place_slots(row_tile, owner_map, out_dev)
    slot_index = target * most_slots + ranking
    vacant_label = jnp.stack(
        [jnp.full((slot_total,), out_dev, jnp.int32), jnp.zeros((slot_total,), jnp.int32)], axis=1
    )
    label_out = vacant_label.at[slot_index].set(jnp.stack([local_row, contraction], axis=1))
    packed = jnp.zeros((wide_count, 8, 128), jnp.int32).at[:, 0, :2 * most_slots].set(
        label_out.reshape(wide_count, 2 * most_slots)
    )
    grp_count = lax.axis_size("grp")
    pieces = [panel] + [
        lax.ppermute(panel, "grp", [(j, (j + shift) % grp_count) for j in range(grp_count)])
        for shift in range(1, grp_count)
    ]
    gathered = jnp.concatenate(pieces, axis=0)
    panel_tiles = gathered.reshape(gathered.shape[0] // tile_side, tile_side, gathered.shape[1])
    band = tile_side * 5 // 8
    picks = []
    for rank in range(most_slots):
        chunk_index = jnp.where(ranking == rank, target, wide_count)
        picks.append(jnp.full((wide_count,), tile_dev, jnp.int32).at[chunk_index].set(
            jnp.arange(tile_dev, dtype=jnp.int32), mode="drop"
        ))
    first = jnp.take(tiles, picks[0], axis=0, mode="clip")
    upper_out = jnp.take(tiles[:, :band, :], picks[1], axis=0, mode="clip")
    upper_out, packed = lax.optimization_barrier((upper_out, packed))
    packed = swap_labels(packed, wide_count)
    upper_out, packed = lax.optimization_barrier((upper_out, packed))
    arrived_labels = packed[:, 0, :2 * most_slots].reshape(wide_count, most_slots, 2)
    held = panel.shape[0] // tile_side
    owner = arrived_labels[..., 1] // held
    shift = lax.rem(lax.axis_index("grp") - owner + grp_count, grp_count)
    arrived_labels = arrived_labels.at[..., 1].set(shift * held + arrived_labels[..., 1] % held)
    lower_out = jnp.take(tiles[:, band:, :], picks[1], axis=0, mode="clip")

    schedules = [slot_order(arrived_labels[:, rank, :], out_dev) for rank in range(most_slots)]

    def exchange(block):
        return lax.all_to_all(block, "wide", split_axis=0, concat_axis=0, tiled=True)

    zero = jnp.zeros((out_dev, tile_side, gathered.shape[1]), jnp.float32)
    whole = add_products(exchange(first), schedules[0], panel_tiles, zero)
    upper = add_products(exchange(upper_out), schedules[1], panel_tiles, whole[:, :band, :])
    lower_out, whole = lax.optimization_barrier((lower_out, whole))
    arrived = exchange(lower_out)
    upper = ring_sum(upper, lax.axis_size("grp"), 0)
    lower = add_products(arrived, schedules[1], panel_tiles, whole[:, band:, :])
    lower = ring_sum(lower, lax.axis_size("grp"), 1)
    summed = jnp.concatenate([upper, lower], axis=1)
    return summed.reshape(out_dev * tile_side, gathered.shape[1])


def solution(mesh):
    return jax.shard_map(
        per_device,
        mesh=mesh,
        in_specs=(
            P(("grp", "wide"), None, None),
            P(("grp", "wide")),
            P(("grp", "wide")),
            P(),
            P("grp", None),
        ),
        out_specs=P("wide", None),
        check_vma=False,
    )
```
